32 devices in a mesh: dp: 8 (over z, y), section: 4 (over x, core).
Axes of the slice: x: 2, y: 2, z: 4, core: 2. Of those that a mesh axis runs over, the one named last changes fastest.
Arguments:
- tiles: bfloat16 [128, 4, 128, 256], P(('dp', 'section')), may hold values from -6 to 6
- out_grad: bfloat16 [128, 4, 128, 256], P(('dp', 'section')), may hold values from -6 to 6
- style: float32 [128, 256], P(('dp', 'section')), may hold values from 0.3 to 3
- weight: bfloat16 [2304, 256], P('dp'), may hold values from -0.125 to 0.125
- tile_counts: int32 [32], P(('dp', 'section')), may hold values from 1 to 4, as said below
- crop_first: int32 [128], P(('dp', 'section')), may hold values 0 or 1
Outputs:
- tile_grad: bfloat16 [128, 4, 128, 256], P(('dp', 'section'))
- weight_grad: float32 [2304, 256], P('dp')
The draws below stay inside these ranges and needn't reach their ends.
Inputs may be any that keep to these rules, and one draw needn't show every extreme that they name: `tile_counts`: live tile slots of each device; some device has 4 and some has 1.
All inputs are finite; a program needn't handle non-finite values. No bound on the sum of `crop_first` on one device may be relied on, other than what follows from the above.
Results may differ from the reference program's by a relative error of at most 0.005.
Values may be sent and summed in bfloat16 or wider, within the bound.
A program may use at most 64 MiB of HBM per device.

```python
import math
import jax
import jax.numpy as jnp
from jax import lax

C = 256
TILE_W = 128
TILE_ROWS = 4
SLOTS = 4
NDEV = 32
TILES_ALL = 128


def draw_tile_counts(key, part):
    draws = jax.random.randint(key, (NDEV,), 0, 16)
    counts = 1 + draws * draws * SLOTS // 256
    counts = counts.at[0].set(SLOTS)
    counts = counts.at[1].set(1)
    return counts.astype(jnp.int32)


def plant(array, stream_key, low, top_value):
    longest = array.shape.index(max(array.shape))
    spots = []
    for shift in (0, 1):
        where = [jax.random.randint(jax.random.fold_in(stream_key, axis), (), 0, length) for axis, length in enumerate(array.shape)]
        where[longest] = (where[longest] + shift) % array.shape[longest]
        spots.append(tuple(where))
    return array.at[spots[0]].set(low).at[spots[1]].set(top_value)


def levels(key, extent, cuts, smallest, high):
    def one(position, parts):
        steps = jax.random.uniform(jax.random.fold_in(jax.random.fold_in(key, 6), position), (parts,), jnp.float32, smallest / len(cuts), high / len(cuts))
        return jnp.repeat(jnp.exp(steps), extent[position] // parts).reshape((-1,) + (1,) * (len(extent) - position - 1))

    loudness = one(*cuts[0])
    for cut in cuts[1:]:
        loudness = loudness * one(*cut)
    return loudness


def centred(stream_key, extent, width, limit, pieces=(), held_as=jnp.bfloat16):
    entries = width * jax.random.normal(stream_key, extent, jnp.float32)
    if pieces:
        entries = entries * levels(stream_key, extent, pieces, -0.22, 0.18)
    return jnp.clip(entries, -limit, limit).astype(held_as)


def setup_inputs(seed: int = 0) -> dict:
    streams_of = jax.random.split(jax.random.key(seed), 7)
    return {
        "tiles": centred(streams_of[0], (TILES_ALL, TILE_ROWS, TILE_W, C), 1.0, 6.0, ((0, 32),)),
        "out_grad": centred(streams_of[1], (TILES_ALL, TILE_ROWS, TILE_W, C), 1.0, 6.0, ((0, 32),)),
        "style": jnp.clip(jnp.exp(math.log(3.0) - 2.3025851 * jax.random.uniform(streams_of[2], (TILES_ALL, C), jnp.float32) ** levels(streams_of[2], (TILES_ALL, C), ((0, 32),), -0.2, 0.2)), 0.3, 3.0),
        "weight": centred(streams_of[3], (9 * C, C), (9 * C) ** -0.5, 0.125, ((0, 8),)),
        "tile_counts": draw_tile_counts(jax.random.fold_in(streams_of[6], 71), 0),
        "crop_first": plant((jax.random.randint(streams_of[5], (TILES_ALL,), 0, 4) < 1).astype(jnp.int32), jax.random.fold_in(streams_of[5], 1), 0, 1),
    }


def tile_block(modulated, scaled, out_grad, style, live, demod, top, bottom, w_taps):
    rows = modulated.shape[1]
    cols = modulated.shape[2]
    w_float = w_taps.astype(jnp.float32)
    ext_mod = jnp.concatenate([top[:, 0][:, None], modulated, bottom[:, 0][:, None]], axis=1)
    ext_grad = jnp.concatenate([top[:, 1][:, None], scaled, bottom[:, 1][:, None]], axis=1)
    pad_mod = jnp.pad(ext_mod, ((0, 0), (0, 0), (1, 1), (0, 0))).astype(jnp.float32)
    pad_grad = jnp.pad(ext_grad, ((0, 0), (0, 0), (1, 1), (0, 0))).astype(jnp.float32)
    scaled_f = scaled.astype(jnp.float32)
    raw_out = jnp.zeros(out_grad.shape, jnp.float32)
    grad_in = jnp.zeros(modulated.shape, jnp.float32)
    mains = []
    for row_off in range(3):
        for col_off in range(3):
            tap = row_off * 3 + col_off
            window = pad_mod[:, row_off:row_off + rows, col_off:col_off + cols, :]
            raw_out = raw_out + jnp.einsum('trpi,io->trpo', window, w_float[tap])
            back = pad_grad[:, 2 - row_off:2 - row_off + rows, 2 - col_off:2 - col_off + cols, :]
            grad_in = grad_in + jnp.einsum('trpo,io->trpi', back, w_float[tap])
            mains.append(jnp.einsum('trpi,trpo->io', window, scaled_f))
    tile_grad = (grad_in * style[:, None, None, :]).astype(jnp.bfloat16)
    demod_dot = live[:, None] * demod ** 3 * lax.optimization_barrier(jnp.sum(out_grad.astype(jnp.float32) * raw_out, axis=(1, 2)))
    coupling = jnp.dot((style * style).T, demod_dot, precision=lax.Precision.HIGHEST)
    term = jnp.stack(mains) - w_float * coupling[None]
    return (tile_grad, term)

def reference(tiles, out_grad, style, weight, tile_counts, crop_first):
    w_taps = weight.reshape(9, C, C)
    w_float = w_taps.astype(jnp.float32)
    w_square = lax.optimization_barrier(jnp.sum(w_float * w_float, axis=0))
    scale = 1.0 / (TILES_ALL * TILE_ROWS * TILE_W) ** 0.5
    slot_ids = jnp.arange(SLOTS, dtype=jnp.int32)
    live_d = (slot_ids[None, :] < tile_counts[:, None]).astype(jnp.float32)
    live = live_d.reshape(TILES_ALL)
    demod = lax.rsqrt(jnp.dot(style * style, w_square, precision=lax.Precision.HIGHEST) + 1e-08)
    modulated = (tiles.astype(jnp.float32) * style[:, None, None, :]).astype(jnp.bfloat16)
    scaled = (out_grad.astype(jnp.float32) * demod[:, None, None, :] * live[:, None, None, None]).astype(jnp.bfloat16)
    mod_d = modulated.reshape(NDEV, SLOTS, TILE_ROWS, TILE_W, C)
    sc_d = scaled.reshape(NDEV, SLOTS, TILE_ROWS, TILE_W, C)
    first_d = crop_first.reshape(NDEV, SLOTS)
    edge = jnp.stack([mod_d[:, :, -1], sc_d[:, :, -1]], axis=2)
    head = jnp.stack([mod_d[:, :, 0], sc_d[:, :, 0]], axis=2)
    dev_ids = jnp.arange(NDEV, dtype=jnp.int32)
    last_live = edge[dev_ids, (tile_counts - 1).astype(jnp.int32)]
    zero_row = jnp.zeros((1, 2, TILE_W, C), jnp.bfloat16)
    recv_top = jnp.concatenate([zero_row, last_live[:-1]], axis=0)
    first_sent = head[:, 0] * (1 - first_d[:, 0]).astype(jnp.bfloat16)[:, None, None, None]
    recv_bot = jnp.concatenate([first_sent[1:], zero_row], axis=0)
    zero_slot = jnp.zeros((NDEV, 1, 2, TILE_W, C), jnp.bfloat16)
    top_local = jnp.concatenate([zero_slot, edge[:, :-1]], axis=1)
    top_mask = ((live_d > 0) & (first_d == 0)).astype(jnp.bfloat16)
    top = jnp.where((slot_ids == 0)[None, :, None, None, None], recv_top[:, None], top_local) * top_mask[:, :, None, None, None]
    next_link = jnp.concatenate([live_d[:, 1:] * (1 - first_d[:, 1:]).astype(jnp.float32), jnp.zeros((NDEV, 1), jnp.float32)], axis=1)
    bot_local = jnp.concatenate([head[:, 1:], zero_slot], axis=1) * next_link.astype(jnp.bfloat16)[:, :, None, None, None]
    is_last = slot_ids[None, :] == (tile_counts - 1)[:, None]
    bottom = jnp.where(is_last[:, :, None, None, None], recv_bot[:, None], bot_local)

    def one_device(total, inputs):
        d_mod, d_sc, d_grad, d_style, d_live, d_demod, d_top, d_bot = inputs
        grads, term = tile_block(d_mod, d_sc, d_grad, d_style, d_live, d_demod, d_top, d_bot, w_taps)
        return (total + term, grads)
    init = jnp.zeros((9, C, C), jnp.float32)
    total, grads = lax.scan(one_device, init, (mod_d, sc_d, out_grad.reshape(NDEV, SLOTS, TILE_ROWS, TILE_W, C), style.reshape(NDEV, SLOTS, C), live_d, demod.reshape(NDEV, SLOTS, C), top, bottom))
    tile_grad = grads.reshape(TILES_ALL, TILE_ROWS, TILE_W, C)
    weight_grad = (total * scale).reshape(9 * C, C)
    return (tile_grad, weight_grad)
```

```python
import functools

import jax
import jax.numpy as jnp
from jax import lax
from jax.experimental import pallas as pl
from jax.experimental.pallas import tpu as pltpu
from jax.sharding import PartitionSpec as P


def from_behind(value, axis, steps):
    count = lax.axis_size(axis)
    leading, last = (max(0, -steps), min(count, count - steps))
    return lax.ppermute(value, axis, [(source, source + steps) for source in range(leading, last)])


def tile_block(modulated, scaled, out_grad, style, live, demod, top, bottom, w_taps):
    rows = modulated.shape[1]
    cols = modulated.shape[2]
    ext_mod = jnp.concatenate([top[:, 0][:, None], modulated, bottom[:, 0][:, None]], axis=1)
    ext_grad = jnp.concatenate([top[:, 1][:, None], scaled, bottom[:, 1][:, None]], axis=1)
    pad_mod = jnp.pad(ext_mod, ((0, 0), (0, 0), (1, 1), (0, 0)))
    pad_grad = jnp.pad(ext_grad, ((0, 0), (0, 0), (1, 1), (0, 0)))
    raw_out = jnp.zeros(out_grad.shape, jnp.float32)
    grad_in = jnp.zeros(modulated.shape, jnp.float32)
    mains = []
    for row_off in range(3):
        for col_off in range(3):
            tap = row_off * 3 + col_off
            window = pad_mod[:, row_off : row_off + rows, col_off : col_off + cols, :]
            raw_out = raw_out + jnp.einsum(
                "trpi,io->trpo", window, w_taps[tap], preferred_element_type=jnp.float32
            )
            back = pad_grad[
                :, 2 - row_off : 2 - row_off + rows, 2 - col_off : 2 - col_off + cols, :
            ]
            grad_in = grad_in + jnp.einsum(
                "trpo,io->trpi", back, w_taps[tap], preferred_element_type=jnp.float32
            )
            mains.append(
                jnp.einsum("trpi,trpo->io", window, scaled, preferred_element_type=jnp.float32)
            )
    tile_grad = (grad_in * style[:, None, None, :]).astype(jnp.bfloat16)
    demod_dot = (
        live[:, None] * demod**3 * jnp.sum(out_grad.astype(jnp.float32) * raw_out, axis=(1, 2))
    )
    coupling = jnp.dot((style * style).T, demod_dot, precision=lax.Precision.HIGHEST)
    term = jnp.stack(mains) - w_taps.astype(jnp.float32) * coupling[None]
    return (tile_grad, term)


def per_device(tiles, out_grad, style, weight, tile_counts, crop_first):
    channels = weight.shape[1]
    slot_count = tiles.shape[0]
    devices = lax.axis_size("dp") * lax.axis_size("section")
    scale = 1.0 / (slot_count * devices * tiles.shape[1] * tiles.shape[2]) ** 0.5
    full_weight = lax.all_gather(weight, "dp", axis=0, tiled=True)
    w_taps = full_weight.reshape(9, channels, channels)
    w_float = w_taps.astype(jnp.float32)
    w_square = jnp.sum(w_float * w_float, axis=0)
    count = tile_counts[0]
    slot_ids = jnp.arange(slot_count, dtype=jnp.int32)
    live = (slot_ids < count).astype(jnp.float32)
    demod = lax.rsqrt(jnp.dot(style * style, w_square, precision=lax.Precision.HIGHEST) + 1e-08)
    modulated = (tiles.astype(jnp.float32) * style[:, None, None, :]).astype(jnp.bfloat16)
    scaled = (
        out_grad.astype(jnp.float32) * demod[:, None, None, :] * live[:, None, None, None]
    ).astype(jnp.bfloat16)
    edge = jnp.stack([modulated[:, -1], scaled[:, -1]], axis=1)
    head = jnp.stack([modulated[:, 0], scaled[:, 0]], axis=1)
    last_live = lax.dynamic_index_in_dim(edge, count - 1, 0, keepdims=False)
    recv_top = from_behind(last_live, ("dp", "section"), 1)
    first_sent = head[0] * (1 - crop_first[0]).astype(jnp.bfloat16)
    recv_bot = from_behind(first_sent, ("dp", "section"), -1)
    zero_slot = jnp.zeros((1,) + edge.shape[1:], jnp.bfloat16)
    top_local = jnp.concatenate([zero_slot, edge[:-1]], axis=0)
    top_mask = ((live > 0) & (crop_first == 0)).astype(jnp.bfloat16)
    top = (
        jnp.where((slot_ids == 0)[:, None, None, None], recv_top[None], top_local)
        * top_mask[:, None, None, None]
    )
    next_link = jnp.concatenate(
        [live[1:] * (1 - crop_first[1:]).astype(jnp.float32), jnp.zeros((1,), jnp.float32)], axis=0
    )
    bot_local = (
        jnp.concatenate([head[1:], zero_slot], axis=0)
        * next_link.astype(jnp.bfloat16)[:, None, None, None]
    )
    bottom = jnp.where((slot_ids == count - 1)[:, None, None, None], recv_bot[None], bot_local)
    tile_grad, term = tile_block(
        modulated, scaled, out_grad, style, live, demod, top, bottom, w_taps
    )
    flat_term = (term * scale).reshape(9 * channels, channels)
    shard = lax.psum_scatter(flat_term, "dp", scatter_dimension=0, tiled=True)
    weight_grad = lax.psum(shard, "section")
    return (tile_grad, weight_grad)


MESH = pl.DeviceIdType.MESH
F32 = jnp.float32
BF16 = jnp.bfloat16


def rolled(value, steps):
    wide = value.shape[0]
    place = lax.broadcasted_iota(jnp.int32, value.shape, 0)
    moved = pltpu.roll(value, steps % wide, 0)
    keep = (place >= steps) if steps > 0 else (place < wide + steps)
    return jnp.where(keep, moved, 0.0)


def fold(value):
    return value.reshape(value.shape[0] // 8, 8, value.shape[1]).sum(axis=0)


def fused_kernel(
    dps, secs, scale,
    count_ref, first_ref, tiles_ref, g_ref, style_ref, w_ref,
    tg_ref, wg_ref,
    wfull, halo_out, halo_in, hsty_out, hsty_in, sty, styt, modt, gcat, mains, wcat, scaled,
    coup, facts, terms, crossing, pair_in, summed, rs_in, line_out, line_in, fin,
    w_ss, w_rs, f_ss, f_rs, h_ss, h_rs, p_ss, p_rs, r_ss, r_rs, l_ss, l_rs, a_ss, a_rs,
):
    slots, rows, cols, ch = tiles_ref.shape
    block = w_ref.shape[0]
    half = block // 2
    lanes = ch // 2
    d = lax.axis_index("dp")
    s = lax.axis_index("section")
    n = d * secs + s
    total = dps * secs
    core = s % 2
    xc = s // 2
    count = count_ref[0]

    def remote(src, dst, ss, rs, dp, sec):
        return pltpu.make_async_remote_copy(
            src_ref=src, dst_ref=dst, send_sem=ss, recv_sem=rs,
            device_id=(dp, sec), device_id_type=MESH,
        )

    zs = dps // 2
    z = d // 2
    y = d % 2

    def at(dz, dy, dx, dc):
        return ((z + dz) % zs) * 2 + (y + dy) % 2, ((xc + dx) % 2) * 2 + (core + dc) % 2

    after, before = (n + 1) % total, (n + total - 1) % total
    plane = ((1, 1), (1, 0), (0, 1))
    barrier = pltpu.get_barrier_semaphore()
    peers = [(after // secs, after % secs), (before // secs, before % secs)]
    peers += [at(k, 0, 0, 0) for k in range(1, zs)] + [at(0, dy, dx, 0) for dy, dx in plane]
    peers += [at(0, 0, 0, 1), at(0, 0, 1, 1)]
    for peer in peers:
        pl.semaphore_signal(barrier, inc=1, device_id=peer, device_id_type=MESH)

    row_t = tiles_ref[0, rows - 1].astype(F32)
    row_g = g_ref[0, rows - 1].astype(F32)
    row_s = style_ref[0:1, :]
    for t in range(1, slots):
        here = count - 1 == t
        row_t = jnp.where(here, tiles_ref[t, rows - 1].astype(F32), row_t)
        row_g = jnp.where(here, g_ref[t, rows - 1].astype(F32), row_g)
        row_s = jnp.where(here, style_ref[t : t + 1, :], row_s)
    halo_out[0, 0] = (row_t * row_s).astype(BF16)
    halo_out[0, 1] = row_g.astype(BF16)
    hsty_out[0] = jnp.broadcast_to(row_s, (8, ch))
    open_first = (1 - first_ref[0]).astype(F32)
    row_s = style_ref[0:1, :]
    halo_out[1, 0] = (tiles_ref[0, 0].astype(F32) * row_s * open_first).astype(BF16)
    halo_out[1, 1] = (g_ref[0, 0].astype(F32) * open_first).astype(BF16)
    hsty_out[1] = jnp.broadcast_to(row_s, (8, ch))
    pl.semaphore_wait(barrier, len(peers))
    ways = ((after, n < total - 1, n > 0), (before, n > 0, n < total - 1))
    halos = []
    for way, (to, _, _) in enumerate(ways):
        halos.append([
            remote(halo_out.at[way], halo_in.at[way], h_ss.at[way], h_rs.at[way], to // secs, to % secs),
            remote(hsty_out.at[way], hsty_in.at[way], h_ss.at[2 + way], h_rs.at[2 + way], to // secs, to % secs),
        ])
    for way, (_, gives, takes) in enumerate(ways):
        @pl.when(gives)
        def _(way=way):
            for copy in halos[way]:
                copy.start()

        @pl.when(jnp.logical_not(takes))
        def _(way=way):
            halo_in[way] = jnp.zeros_like(halo_in[way])
            hsty_in[way] = jnp.zeros_like(hsty_in[way])

    def w_rows(owner, which):
        return wfull.at[pl.ds(pl.multiple_of(block * owner + half * which, 16), half), :]

    mine = w_ref.at[pl.ds(pl.multiple_of(half * core, 16), half), :]
    sends = []

    def send(copy):
        copy.start()
        sends.append(copy)

    for k in range(1, zs):
        send(remote(mine, w_rows(d, core), w_ss.at[k - 1], w_rs.at[k - 1], *at(k, 0, 0, 0)))
    send(remote(mine, w_rows(d, core), w_ss.at[zs - 1], w_rs.at[zs - 1], *at(0, 1, 0, 0)))
    wfull[pl.ds(pl.multiple_of(block * d, 16), block), :] = w_ref[...]

    def put_g(row, value):
        gcat[row, :, 0:ch] = rolled(value, -1).astype(BF16)
        gcat[row, :, ch : 2 * ch] = value.astype(BF16)
        gcat[row, :, 2 * ch : 3 * ch] = rolled(value, 1).astype(BF16)

    def prepare(t, carry):
        row_style = style_ref[pl.ds(t, 1), :]
        for r in range(rows):
            value = (tiles_ref[t, r].astype(F32) * row_style).astype(BF16)
            modt[t, :, (r + 1) * cols : (r + 2) * cols] = value.T
            put_g(t * rows + r, g_ref[t, r].astype(F32))
        return carry

    lax.fori_loop(0, slots, prepare, 0)

    live = [(t < count).astype(F32) for t in range(slots)]
    shut = [(first_ref[t] == 0).astype(F32) for t in range(slots)]
    top_on = [live[t] * shut[t] for t in range(slots)]
    top_on[0] = top_on[0] * (n > 0).astype(F32)
    next_on = [live[t + 1] * shut[t + 1] for t in range(slots - 1)]
    last_on = [(count - 1 == t).astype(F32) * (n < total - 1).astype(F32) for t in range(slots)]

    for way, (_, _, takes) in enumerate(ways):
        @pl.when(takes)
        def _(way=way):
            for copy in halos[way]:
                copy.wait_recv()

    sty[...] = jnp.zeros_like(sty)
    sty[0:slots, :] = style_ref[...]
    sty[slots : slots + 1, :] = hsty_in[0, 0:1, :]
    sty[slots + 1 : slots + 2, :] = hsty_in[1, 0:1, :]
    squared = sty[...]
    styt[...] = (squared * squared).T
    put_g(slots * rows, halo_in[0, 1].astype(F32))
    put_g(slots * rows + 1, halo_in[1, 1].astype(F32))
    from_prev = halo_in[0, 0].T.astype(F32)
    from_next = halo_in[1, 0].T.astype(F32)
    for t in range(slots):
        above = from_prev if t == 0 else modt[t - 1, :, rows * cols : (rows + 1) * cols].astype(F32)
        modt[t, :, 0:cols] = (above * top_on[t]).astype(BF16)
        below = from_next * last_on[t]
        if t < slots - 1:
            below = below + modt[t + 1, :, cols : 2 * cols].astype(F32) * next_on[t]
        modt[t, :, (rows + 1) * cols : (rows + 2) * cols] = below.astype(BF16)

    def tile_mains(t, carry):
        right = gcat[pl.ds(t * rows, rows)].reshape(rows * cols, 3 * ch)
        for a in range(3):
            found = jnp.dot(modt[t, :, a * cols : (a + rows) * cols], right, preferred_element_type=F32)
            for b in range(3):
                tap = 3 * a + b
                mains[t, tap * ch : (tap + 1) * ch, :] = found[:, b * ch : (b + 1) * ch]
        return carry

    def w_wait(place, ss, rs, peer):
        remote(place, place, ss, rs, *peer).wait_recv()

    lax.fori_loop(0, 1, tile_mains, 0)
    sibling = at(0, 0, 0, 1)
    other_y = at(0, 1, 0, 0)
    for k in range(1, zs):
        place = w_rows(((z + zs - k) % zs) * 2 + y, core)
        w_wait(place, w_ss.at[k - 1], w_rs.at[k - 1], at(k, 0, 0, 0))
        send(remote(place, place, w_ss.at[zs - 1 + k], w_rs.at[zs - 1 + k], *other_y))
        send(remote(place, place, f_ss.at[k - 1], f_rs.at[k - 1], *sibling))
    lax.fori_loop(1, slots, tile_mains, 0)
    for k in range(zs):
        place = w_rows(((z + zs - k) % zs) * 2 + 1 - y, core)
        w_wait(place, w_ss.at[zs - 1 + k], w_rs.at[zs - 1 + k], other_y)
        send(remote(place, place, f_ss.at[zs - 1 + k], f_rs.at[zs - 1 + k], *sibling))
    for k in range(1, zs):
        place = w_rows(((z + zs - k) % zs) * 2 + y, 1 - core)
        w_wait(place, f_ss.at[k - 1], f_rs.at[k - 1], sibling)
    for k in range(zs):
        place = w_rows(((z + zs - k) % zs) * 2 + 1 - y, 1 - core)
        w_wait(place, f_ss.at[zs - 1 + k], f_rs.at[zs - 1 + k], sibling)

    part = 64
    zero = jnp.zeros((8, ch), F32)

    def sums(k, carry):
        dots, norms = list(carry[0]), list(carry[1])
        square = jnp.zeros((part, ch), F32)
        for tap in range(9):
            here = pl.ds(pl.multiple_of(tap * ch + k * part, part), part)
            wv = wfull[here, :].astype(F32)
            square = square + wv * wv
            for t in range(slots):
                dots[t] = dots[t] + fold(wv * mains[t, here, :])
        columns = styt[pl.ds(pl.multiple_of(k * part, part), part), :]
        for t in range(slots + 2):
            norms[t] = norms[t] + fold(square * columns[:, t : t + 1])
        return tuple(dots), tuple(norms)

    dots, norms = lax.fori_loop(0, ch // part, sums, ((zero,) * slots, (zero,) * (slots + 2)))
    demod = [lax.rsqrt(jnp.sum(v, axis=0, keepdims=True) + 1e-08) for v in norms]
    pull = [
        live[t] * demod[t] * demod[t] * demod[t] * jnp.sum(dots[t], axis=0, keepdims=True) * scale
        for t in range(slots)
    ]
    gain = [demod[t] * live[t] * scale for t in range(slots)]
    for t in range(slots):
        facts[t : t + 1, :] = demod[t] * live[t]

    def couple(k, carry):
        here = pl.ds(pl.multiple_of(k * part, part), part)
        columns = styt[here, :]
        coup[here, :] = sum(columns[:, t : t + 1] * pull[t] for t in range(slots))
        return carry

    lax.fori_loop(0, ch // part, couple, 0)

    chunk = 2 * block

    def term(k, carry):
        here = pl.ds(pl.multiple_of(k * part, part), part)
        inner = pl.ds(pl.multiple_of((k % (ch // part)) * part, part), part)
        value = sum(gain[t] * mains[t, here, :] for t in range(slots))
        value = value - wfull[here, :].astype(F32) * coup[inner, :]
        terms[0, here, :] = value[:, :lanes]
        terms[1, here, :] = value[:, lanes:]
        for h in range(2):
            crossing[h, here, :] = value[:, h * lanes : (h + 1) * lanes].astype(BF16)
        return carry

    steps = chunk // part
    order = list(range(1, zs)) + [0]
    pairs = []
    for i, k in enumerate(order):
        zd = (z + k) % zs
        lax.fori_loop(zd * steps, (zd + 1) * steps, term, 0)
        span = pl.ds(pl.multiple_of(chunk * zd, 64), chunk)
        pairs.append(remote(crossing.at[1 - core, span, :], pair_in.at[span, :], p_ss.at[i], p_rs.at[i], *sibling))
        pairs[i].start()

    def share(zd, dy, dx):
        row = chunk * zd + block * ((y + dy) % 2) + half * ((xc + dx) % 2)
        return pl.ds(pl.multiple_of(row, 16), half)

    shares = []
    for i, k in enumerate(order):
        zd = (z + k) % zs
        pairs[i].wait_recv()

        def add_pair(m, carry):
            here = pl.ds(pl.multiple_of(zd * chunk + m * part, part), part)
            both = terms[core, here, :] + pair_in[here, :].astype(F32)
            terms[core, here, :] = both
            summed[here, :] = both.astype(BF16)
            return carry

        lax.fori_loop(0, steps, add_pair, 0)
        for m, (dy, dx) in enumerate(plane):
            copy = remote(
                summed.at[share(zd, dy, dx), :], rs_in.at[i, m], r_ss.at[3 * i + m], r_rs.at[3 * i + m], *at(0, dy, dx, 0)
            )
            copy.start()
            shares.append(copy)

    for a in range(3):
        for b in range(3):
            tap = 3 * a + b
            wcat[a, :, b * ch : (b + 1) * ch] = wfull[tap * ch : (tap + 1) * ch, :]

    def rescale(t, carry):
        factor = facts[pl.ds(t, 1), :]
        for r in range(rows):
            for b in range(3):
                tap = slice(b * ch, (b + 1) * ch)
                scaled[t, r + 1, :, tap] = (gcat[t * rows + r, :, tap].astype(F32) * factor).astype(BF16)
        return carry

    lax.fori_loop(0, slots, rescale, 0)
    for t in range(slots):
        for b in range(3):
            tap = slice(b * ch, (b + 1) * ch)
            above, factor = (slots * rows, demod[slots]) if t == 0 else (t * rows - 1, demod[t - 1])
            scaled[t, 0, :, tap] = (gcat[above, :, tap].astype(F32) * (factor * top_on[t])).astype(BF16)
            below = gcat[slots * rows + 1, :, tap].astype(F32) * (demod[slots + 1] * last_on[t])
            if t < slots - 1:
                below = below + gcat[(t + 1) * rows, :, tap].astype(F32) * (demod[t + 1] * next_on[t])
            scaled[t, rows + 1, :, tap] = below.astype(BF16)

    def tile_back(t, carry):
        found = None
        for a in range(3):
            left = scaled[t, 2 - a : 2 - a + rows].reshape(rows * cols, 3 * ch)
            more = lax.dot_general(left, wcat[a], (((1,), (1,)), ((), ())), preferred_element_type=F32)
            found = more if found is None else found + more
        found = (found * style_ref[pl.ds(t, 1), :]).astype(BF16)
        tg_ref[t] = found.reshape(rows, cols, ch)
        return carry

    lines = []
    for i, k in enumerate(order):
        lax.fori_loop(i * slots // zs, (i + 1) * slots // zs, tile_back, 0)
        own = terms[core, share((z + k) % zs, 0, 0), :]
        for m in range(3):
            shares[3 * i + m].wait_recv()
            own = own + rs_in[i, m].astype(F32)
        if k:
            line_out[k - 1] = own.astype(BF16)
            lines.append(remote(line_out.at[k - 1], line_in.at[k - 1], l_ss.at[k - 1], l_rs.at[k - 1], *at(k, 0, 0, 0)))
            lines[-1].start()
    for k in range(1, zs):
        lines[k - 1].wait_recv()
        own = own + line_in[k - 1].astype(F32)
    fin[s] = own.astype(BF16)
    gathers = []
    for k in range(1, secs):
        copy = remote(fin.at[s], fin.at[s], a_ss.at[k - 1], a_rs.at[k - 1], d, (s + k) % secs)
        copy.start()
        gathers.append(copy)
    for k in range(1, secs):
        other = fin.at[(s + secs - k) % secs]
        remote(other, other, a_ss.at[k - 1], a_rs.at[k - 1], d, (s + k) % secs).wait_recv()
    for q in range(secs):
        wg_ref[half * (q // 2) : half * (q // 2 + 1), lanes * (q % 2) : lanes * (q % 2 + 1)] = fin[q].astype(F32)
    for way, (_, gives, _) in enumerate(ways):
        @pl.when(gives)
        def _(way=way):
            for copy in halos[way]:
                copy.wait_send()

    for copy in sends + pairs + shares + lines + gathers:
        copy.wait_send()


def store_kernel(tg_ref, wg_ref, tg_out, wg_out, t_sem, w_sem):
    copies = [pltpu.make_async_copy(tg_ref.at[t], tg_out.at[t], t_sem.at[t]) for t in range(tg_ref.shape[0])]
    copies.append(pltpu.make_async_copy(wg_ref, wg_out, w_sem))
    for copy in copies:
        copy.start()
    for copy in copies:
        copy.wait()


def fused(dps, secs, tiles, out_grad, style, weight, tile_counts, crop_first):
    slots, rows, cols, ch = tiles.shape
    block = weight.shape[0]
    half = block // 2
    lanes = ch // 2
    scale = 1.0 / (slots * dps * secs * rows * cols) ** 0.5
    dma = pltpu.SemaphoreType.DMA
    vmem = pl.BlockSpec(memory_space=pltpu.VMEM)
    smem = pl.BlockSpec(memory_space=pltpu.SMEM)
    tg, wg = pl.pallas_call(
        functools.partial(fused_kernel, dps, secs, scale),
        out_shape=(
            pltpu.VMEM(tiles.shape, BF16),
            pltpu.VMEM(weight.shape, F32),
        ),
        in_specs=[smem, smem, vmem, vmem, vmem, vmem],
        out_specs=(vmem, vmem),
        scratch_shapes=[
            pltpu.VMEM((9 * ch, ch), BF16),
            pltpu.VMEM((2, 2, cols, ch), BF16),
            pltpu.VMEM((2, 2, cols, ch), BF16),
            pltpu.VMEM((2, 8, ch), F32),
            pltpu.VMEM((2, 8, ch), F32),
            pltpu.VMEM((128, ch), F32),
            pltpu.VMEM((ch, 128), F32),
            pltpu.VMEM((slots, ch, (rows + 2) * cols), BF16),
            pltpu.VMEM((slots * rows + 2, cols, 3 * ch), BF16),
            pltpu.VMEM((slots, 9 * ch, ch), F32),
            pltpu.VMEM((3, ch, 3 * ch), BF16),
            pltpu.VMEM((slots, rows + 2, cols, 3 * ch), BF16),
            pltpu.VMEM((ch, ch), F32),
            pltpu.VMEM((8, ch), F32),
            pltpu.VMEM((2, 9 * ch, lanes), F32),
            pltpu.VMEM((2, 9 * ch, lanes), BF16),
            pltpu.VMEM((9 * ch, lanes), BF16),
            pltpu.VMEM((9 * ch, lanes), BF16),
            pltpu.VMEM((dps // 2, 3, half, lanes), BF16),
            pltpu.VMEM((dps // 2 - 1, half, lanes), BF16),
            pltpu.VMEM((dps // 2 - 1, half, lanes), BF16),
            pltpu.VMEM((secs, half, lanes), BF16),
            dma((dps - 1,)), dma((dps - 1,)), dma((dps - 1,)), dma((dps - 1,)),
            dma((4,)), dma((4,)), dma((dps // 2,)), dma((dps // 2,)),
            dma((3 * dps // 2,)), dma((3 * dps // 2,)), dma((dps // 2 - 1,)), dma((dps // 2 - 1,)),
            dma((secs - 1,)), dma((secs - 1,)),
        ],
        compiler_params=pltpu.CompilerParams(collective_id=0, has_side_effects=True, vmem_limit_bytes=56 * 1024 * 1024),
        name="fused_backward",
    )(tile_counts, crop_first, tiles, out_grad, style, weight)
    hbm = pl.BlockSpec(memory_space=pl.ANY)
    return pl.pallas_call(
        store_kernel,
        out_shape=(
            jax.ShapeDtypeStruct(tiles.shape, BF16),
            jax.ShapeDtypeStruct(weight.shape, F32),
        ),
        in_specs=[vmem, vmem],
        out_specs=(hbm, hbm),
        scratch_shapes=[dma((slots,)), dma],
        compiler_params=pltpu.CompilerParams(has_side_effects=True, vmem_limit_bytes=1024 * 1024),
        name="store_out",
    )(tg, wg)


def solution(mesh):
    placed = (
        P(("dp", "section"), None, None, None),
        P(("dp", "section"), None, None, None),
        P(("dp", "section"), None),
        P("dp", None),
        P(("dp", "section")),
        P(("dp", "section")),
    )
    dps, secs = mesh.shape["dp"], mesh.shape["section"]

    def body(tiles, out_grad, style, weight, tile_counts, crop_first):
        args = (tiles, out_grad, style, weight, tile_counts, crop_first)
        if weight.shape[0] % 32 == 0 and secs == 4 and dps % 2 == 0:
            return fused(dps, secs, *args)
        return per_device(*args)

    return jax.shard_map(
        body,
        mesh=mesh,
        in_specs=placed,
        out_specs=(P(("dp", "section"), None, None, None), P("dp", None)),
        check_vma=False,
    )
```

```python
import functools

import jax
import jax.numpy as jnp
from jax import lax
from jax.experimental import pallas as pl
from jax.experimental.pallas import tpu as pltpu
from jax.sharding import PartitionSpec as P


def from_behind(value, axis, steps):
    count = lax.axis_size(axis)
    leading, last = (max(0, -steps), min(count, count - steps))
    return lax.ppermute(value, axis, [(source, source + steps) for source in range(leading, last)])


def tile_block(modulated, scaled, out_grad, style, live, demod, top, bottom, w_taps):
    rows = modulated.shape[1]
    cols = modulated.shape[2]
    ext_mod = jnp.concatenate([top[:, 0][:, None], modulated, bottom[:, 0][:, None]], axis=1)
    ext_grad = jnp.concatenate([top[:, 1][:, None], scaled, bottom[:, 1][:, None]], axis=1)
    pad_mod = jnp.pad(ext_mod, ((0, 0), (0, 0), (1, 1), (0, 0)))
    pad_grad = jnp.pad(ext_grad, ((0, 0), (0, 0), (1, 1), (0, 0)))
    raw_out = jnp.zeros(out_grad.shape, jnp.float32)
    grad_in = jnp.zeros(modulated.shape, jnp.float32)
    mains = []
    for row_off in range(3):
        for col_off in range(3):
            tap = row_off * 3 + col_off
            window = pad_mod[:, row_off : row_off + rows, col_off : col_off + cols, :]
            raw_out = raw_out + jnp.einsum(
                "trpi,io->trpo", window, w_taps[tap], preferred_element_type=jnp.float32
            )
            back = pad_grad[
                :, 2 - row_off : 2 - row_off + rows, 2 - col_off : 2 - col_off + cols, :
            ]
            grad_in = grad_in + jnp.einsum(
                "trpo,io->trpi", back, w_taps[tap], preferred_element_type=jnp.float32
            )
            mains.append(
                jnp.einsum("trpi,trpo->io", window, scaled, preferred_element_type=jnp.float32)
            )
    tile_grad = (grad_in * style[:, None, None, :]).astype(jnp.bfloat16)
    demod_dot = (
        live[:, None] * demod**3 * jnp.sum(out_grad.astype(jnp.float32) * raw_out, axis=(1, 2))
    )
    coupling = jnp.dot((style * style).T, demod_dot, precision=lax.Precision.HIGHEST)
    term = jnp.stack(mains) - w_taps.astype(jnp.float32) * coupling[None]
    return (tile_grad, term)


def per_device(tiles, out_grad, style, weight, tile_counts, crop_first):
    channels = weight.shape[1]
    slot_count = tiles.shape[0]
    devices = lax.axis_size("dp") * lax.axis_size("section")
    scale = 1.0 / (slot_count * devices * tiles.shape[1] * tiles.shape[2]) ** 0.5
    full_weight = lax.all_gather(weight, "dp", axis=0, tiled=True)
    w_taps = full_weight.reshape(9, channels, channels)
    w_float = w_taps.astype(jnp.float32)
    w_square = jnp.sum(w_float * w_float, axis=0)
    count = tile_counts[0]
    slot_ids = jnp.arange(slot_count, dtype=jnp.int32)
    live = (slot_ids < count).astype(jnp.float32)
    demod = lax.rsqrt(jnp.dot(style * style, w_square, precision=lax.Precision.HIGHEST) + 1e-08)
    modulated = (tiles.astype(jnp.float32) * style[:, None, None, :]).astype(jnp.bfloat16)
    scaled = (
        out_grad.astype(jnp.float32) * demod[:, None, None, :] * live[:, None, None, None]
    ).astype(jnp.bfloat16)
    edge = jnp.stack([modulated[:, -1], scaled[:, -1]], axis=1)
    head = jnp.stack([modulated[:, 0], scaled[:, 0]], axis=1)
    last_live = lax.dynamic_index_in_dim(edge, count - 1, 0, keepdims=False)
    recv_top = from_behind(last_live, ("dp", "section"), 1)
    first_sent = head[0] * (1 - crop_first[0]).astype(jnp.bfloat16)
    recv_bot = from_behind(first_sent, ("dp", "section"), -1)
    zero_slot = jnp.zeros((1,) + edge.shape[1:], jnp.bfloat16)
    top_local = jnp.concatenate([zero_slot, edge[:-1]], axis=0)
    top_mask = ((live > 0) & (crop_first == 0)).astype(jnp.bfloat16)
    top = (
        jnp.where((slot_ids == 0)[:, None, None, None], recv_top[None], top_local)
        * top_mask[:, None, None, None]
    )
    next_link = jnp.concatenate(
        [live[1:] * (1 - crop_first[1:]).astype(jnp.float32), jnp.zeros((1,), jnp.float32)], axis=0
    )
    bot_local = (
        jnp.concatenate([head[1:], zero_slot], axis=0)
        * next_link.astype(jnp.bfloat16)[:, None, None, None]
    )
    bottom = jnp.where((slot_ids == count - 1)[:, None, None, None], recv_bot[None], bot_local)
    tile_grad, term = tile_block(
        modulated, scaled, out_grad, style, live, demod, top, bottom, w_taps
    )
    flat_term = (term * scale).reshape(9 * channels, channels)
    shard = lax.psum_scatter(flat_term, "dp", scatter_dimension=0, tiled=True)
    weight_grad = lax.psum(shard, "section")
    return (tile_grad, weight_grad)


MESH = pl.DeviceIdType.MESH
F32 = jnp.float32
BF16 = jnp.bfloat16


def rolled(value, steps):
    wide = value.shape[0]
    place = lax.broadcasted_iota(jnp.int32, value.shape, 0)
    moved = pltpu.roll(value, steps % wide, 0)
    keep = (place >= steps) if steps > 0 else (place < wide + steps)
    return jnp.where(keep, moved, 0.0)


def fold(value):
    return value.reshape(value.shape[0] // 8, 8, value.shape[1]).sum(axis=0)


def fused_kernel(
    dps, secs, scale,
    count_hbm, first_hbm, tiles_hbm, g_hbm, style_hbm, w_hbm,
    tg_ref, wg_ref,
    count_ref, first_ref, tiles_ref, g_ref, style_ref, wfull, halo_out, halo_in, hdem_out, hdem_in, wsq, sq_all, norm_out, norm_in,
    pull_all, coup, modt, gcat, mains, wcat, scaled, facts, terms, crossing, pair_in, summed, rs_in,
    line_out, line_in, fin,
    in_sem, h_ss, h_rs, sq_ss, sq_rs, sx_ss, sx_rs, nm_ss, nm_rs, pl_ss, pl_rs, px_ss, px_rs,
    wz_ss, wz_rs, wo_ss, wo_rs, wp_ss, wp_rs, sw_ss, sw_rs, p_ss, p_rs, r_ss, r_rs, l_ss, l_rs, a_ss, a_rs,
):
    slots, rows, cols, ch = tiles_ref.shape
    block = w_hbm.shape[0]
    half = block // 2
    lanes = ch // 2
    d = lax.axis_index("dp")
    s = lax.axis_index("section")
    n = d * secs + s
    total = dps * secs
    core = s % 2
    xc = s // 2
    zs = dps // 2
    z = d // 2
    y = d % 2

    def remote(src, dst, ss, rs, dp, sec):
        return pltpu.make_async_remote_copy(
            src_ref=src, dst_ref=dst, send_sem=ss, recv_sem=rs,
            device_id=(dp, sec), device_id_type=MESH,
        )

    def at(dz, dy, dx, dc):
        return ((z + dz) % zs) * 2 + (y + dy) % 2, ((xc + dx) % 2) * 2 + (core + dc) % 2

    after, before = (n + 1) % total, (n + total - 1) % total
    plane = ((1, 1), (1, 0), (0, 1))
    sibling = at(0, 0, 0, 1)
    other_y = at(0, 1, 0, 0)
    far = [3 - 3 * (z // 2), 2 - z // 2, z + 1 - 2 * (z % 2)]
    barrier = pltpu.get_barrier_semaphore()
    others = [far[j] * 2 + (y + dy) % 2 for j in range(zs - 1) for dy in (1, 0)] + [z * 2 + 1 - y]
    peers = [(owner, s) for owner in others] + [(d, (s + k) % secs) for k in range(1, secs)]
    peers += [at(0, 1, 1, 0), (after // secs, after % secs), (before // secs, before % secs)]
    for peer in peers:
        pl.semaphore_signal(barrier, inc=1, device_id=peer, device_id_type=MESH)

    mine = pl.ds(pl.multiple_of(block * d, 16), block)
    loads = [
        pltpu.make_async_copy(style_hbm, style_ref, in_sem.at[0]),
        pltpu.make_async_copy(w_hbm.at[:, 0:lanes], wfull.at[0, mine, :], in_sem.at[1]),
        pltpu.make_async_copy(w_hbm.at[:, lanes:ch], wfull.at[1, mine, :], in_sem.at[2]),
        pltpu.make_async_copy(tiles_hbm, tiles_ref, in_sem.at[3]),
        pltpu.make_async_copy(g_hbm, g_ref, in_sem.at[4]),
        pltpu.make_async_copy(count_hbm, count_ref, in_sem.at[5]),
        pltpu.make_async_copy(first_hbm, first_ref, in_sem.at[6]),
    ]
    for load in loads:
        load.start()
    sends = []

    def send(copy):
        copy.start()
        sends.append(copy)

    loads[0].wait()
    square = style_ref[...] * style_ref[...]
    sq_all[s, d, 0:slots, :] = square[:, :lanes]
    sq_all[s, d, slots : 2 * slots, :] = square[:, lanes:]
    pl.semaphore_wait(barrier, len(peers))

    def spread(ref, ss, rs):
        for i, owner in enumerate(others):
            send(remote(ref.at[s, d], ref.at[s, d], ss.at[i], rs.at[d], owner, s))

    def collect(ref, ss, rs):
        for i, owner in enumerate(others):
            remote(ref.at[s, owner], ref.at[s, owner], ss.at[i], rs.at[owner], owner, s).wait_recv()

    spread(sq_all, sq_ss, sq_rs)
    loads[1].wait()
    loads[2].wait()

    def w_part(owner, which):
        return wfull.at[core, pl.ds(pl.multiple_of(block * owner + half * which, 16), half), :]

    for j in range(zs - 1):
        send(remote(w_part(d, xc), w_part(d, xc), wz_ss.at[j], wz_rs.at[z], far[j] * 2 + y, s))
    own_w = wfull.at[core, mine, :]
    send(remote(own_w, own_w, wo_ss.at[0], wo_rs.at[0], *other_y))

    loads[3].wait()
    loads[4].wait()
    loads[5].wait()
    loads[6].wait()
    count = count_ref[0]
    row_t = tiles_ref[0, rows - 1].astype(F32)
    row_g = g_ref[0, rows - 1].astype(F32)
    row_s = style_ref[0:1, :]
    for t in range(1, slots):
        here = count - 1 == t
        row_t = jnp.where(here, tiles_ref[t, rows - 1].astype(F32), row_t)
        row_g = jnp.where(here, g_ref[t, rows - 1].astype(F32), row_g)
        row_s = jnp.where(here, style_ref[t : t + 1, :], row_s)
    halo_out[0, 0] = (row_t * row_s).astype(BF16)
    halo_out[0, 1] = row_g.astype(BF16)
    open_first = (1 - first_ref[0]).astype(F32)
    halo_out[1, 0] = (tiles_ref[0, 0].astype(F32) * style_ref[0:1, :] * open_first).astype(BF16)
    halo_out[1, 1] = (g_ref[0, 0].astype(F32) * open_first).astype(BF16)
    ways = ((after, n < total - 1, n > 0), (before, n > 0, n < total - 1))
    halos = []
    for way, (to, _, _) in enumerate(ways):
        halos.append([
            remote(halo_out.at[way], halo_in.at[way], h_ss.at[way], h_rs.at[way], to // secs, to % secs),
            remote(hdem_out.at[way], hdem_in.at[way], h_ss.at[2 + way], h_rs.at[2 + way], to // secs, to % secs),
        ])
    for way, (_, gives, takes) in enumerate(ways):
        @pl.when(gives)
        def _(way=way):
            halos[way][0].start()

        @pl.when(jnp.logical_not(takes))
        def _(way=way):
            halo_in[way] = jnp.zeros_like(halo_in[way])
            hdem_in[way] = jnp.zeros_like(hdem_in[way])

    for h in range(2):
        w_own = wfull[h, mine, :].astype(F32)
        w_own = w_own * w_own
        folded = jnp.concatenate([w_own[: block - ch] + w_own[ch:], w_own[block - ch : ch]], axis=0)
        wsq[0:ch, h * lanes : (h + 1) * lanes] = folded
        wsq[ch : 2 * ch, h * lanes : (h + 1) * lanes] = folded
    shift = (block * d) % ch

    def put_g(row, value):
        gcat[row, :, 0:ch] = rolled(value, -1).astype(BF16)
        gcat[row, :, ch : 2 * ch] = value.astype(BF16)
        gcat[row, :, 2 * ch : 3 * ch] = rolled(value, 1).astype(BF16)

    def prepare(t, carry):
        row_style = style_ref[pl.ds(t, 1), :]
        for r in range(rows):
            value = (tiles_ref[t, r].astype(F32) * row_style).astype(BF16)
            modt[t, :, (r + 1) * cols : (r + 2) * cols] = value.T
            put_g(t * rows + r, g_ref[t, r].astype(F32))
        return carry

    lax.fori_loop(0, slots, prepare, 0)

    live = [(t < count).astype(F32) for t in range(slots)]
    shut = [(first_ref[t] == 0).astype(F32) for t in range(slots)]
    top_on = [live[t] * shut[t] for t in range(slots)]
    top_on[0] = top_on[0] * (n > 0).astype(F32)
    next_on = [live[t + 1] * shut[t + 1] for t in range(slots - 1)]
    last_on = [(count - 1 == t).astype(F32) * (n < total - 1).astype(F32) for t in range(slots)]

    def tile_mains(taps, t, carry):
        right = gcat[pl.ds(t * rows, rows)].reshape(rows * cols, 3 * ch)
        for a in taps:
            found = jnp.dot(modt[t, :, a * cols : (a + rows) * cols], right, preferred_element_type=F32)
            for b in range(3):
                tap = 3 * a + b
                mains[t, tap * ch : (tap + 1) * ch, :] = found[:, b * ch : (b + 1) * ch]
        return carry

    lax.fori_loop(0, slots, functools.partial(tile_mains, (1,)), 0)

    def w_forward(j):
        place = w_part(far[j] * 2 + y, xc)
        remote(place, place, wz_ss.at[j], wz_rs.at[far[j]], far[j] * 2 + y, s).wait_recv()
        for m, (dy, dx) in enumerate(plane):
            send(remote(place, place, wp_ss.at[3 * j + m], wp_rs.at[3 * far[j] + m], *at(0, dy, dx, 0)))

    w_forward(2)
    collect(sq_all, sq_ss, sq_rs)
    wide = dps * 2 * slots
    squares = sq_all[s].reshape(wide, lanes)
    aligned = wsq[pl.ds(pl.multiple_of(ch - shift, 16), ch), :]
    low = jnp.dot(squares, aligned[:lanes], precision=lax.Precision.HIGHEST, preferred_element_type=F32)
    high = jnp.dot(squares, aligned[lanes:], precision=lax.Precision.HIGHEST, preferred_element_type=F32)
    both = low + pltpu.roll(high, wide - slots, 0)
    upper = lax.broadcasted_iota(jnp.int32, (wide, lanes), 0) % (2 * slots) < slots
    packed = jnp.where(upper, both[:, :lanes], pltpu.roll(both[:, lanes:], slots, 0))
    norm_out[...] = packed.reshape(dps, 2 * slots, lanes)
    for i, owner in enumerate(others):
        send(remote(norm_out.at[owner], norm_in.at[d], nm_ss.at[i], nm_rs.at[d], owner, s))
    norm_in[d] = norm_out[d]
    for k in range(1, secs):
        send(remote(sq_all.at[s], sq_all.at[s], sx_ss.at[k - 1], sx_rs.at[k - 1], d, (s + k) % secs))

    w_forward(1)
    for way, (_, _, takes) in enumerate(ways):
        @pl.when(takes)
        def _(way=way):
            halos[way][0].wait_recv()

    put_g(slots * rows, halo_in[0, 1].astype(F32))
    put_g(slots * rows + 1, halo_in[1, 1].astype(F32))
    from_prev = halo_in[0, 0].T.astype(F32)
    from_next = halo_in[1, 0].T.astype(F32)
    for t in range(slots):
        above = from_prev if t == 0 else modt[t - 1, :, rows * cols : (rows + 1) * cols].astype(F32)
        modt[t, :, 0:cols] = (above * top_on[t]).astype(BF16)
        below = from_next * last_on[t]
        if t < slots - 1:
            below = below + modt[t + 1, :, cols : 2 * cols].astype(F32) * next_on[t]
        modt[t, :, (rows + 1) * cols : (rows + 2) * cols] = below.astype(BF16)

    lax.fori_loop(0, 1, functools.partial(tile_mains, (0, 2)), 0)
    w_forward(0)
    lax.fori_loop(1, slots, functools.partial(tile_mains, (0, 2)), 0)

    chunk = 2 * block

    def group(zd, which):
        return wfull.at[which, pl.ds(pl.multiple_of(chunk * zd, 16), chunk), :]

    def other_block(which):
        return wfull.at[which, pl.ds(pl.multiple_of(block * (2 * z + 1 - y), 16), block), :]

    def w_cross(j):
        for m, (dy, dx) in enumerate(plane):
            place = w_part(far[j] * 2 + (y + dy) % 2, (xc + dx) % 2)
            remote(place, place, wp_ss.at[3 * j + m], wp_rs.at[3 * far[j] + m], *at(0, dy, dx, 0)).wait_recv()
        send(remote(group(far[j], core), group(far[j], core), sw_ss.at[j], sw_rs.at[far[j]], *sibling))

    remote(other_block(core), other_block(core), wo_ss.at[0], wo_rs.at[0], *other_y).wait_recv()
    send(remote(other_block(core), other_block(core), sw_ss.at[zs - 1], sw_rs.at[z], *sibling))
    w_cross(2)
    for i, owner in enumerate(others):
        remote(norm_out.at[owner], norm_in.at[owner], nm_ss.at[i], nm_rs.at[owner], owner, s).wait_recv()
    inverse = lax.rsqrt(norm_in[...].sum(axis=0) + 1e-08)
    demod = [
        jnp.concatenate([inverse[t : t + 1, :], inverse[slots + t : slots + t + 1, :]], axis=1)
        for t in range(slots)
    ]
    gain = [demod[t] * live[t] * scale for t in range(slots)]
    for t in range(slots):
        facts[t : t + 1, :] = demod[t] * live[t]

    last = demod[0]
    for t in range(1, slots):
        last = jnp.where(count - 1 == t, demod[t], last)
    hdem_out[0] = jnp.broadcast_to(last, (8, ch))
    hdem_out[1] = jnp.broadcast_to(demod[0], (8, ch))
    for way, (_, gives, _) in enumerate(ways):
        @pl.when(gives)
        def _(way=way):
            halos[way][1].start()

    part = 64
    steps = chunk // part

    def term(k, carry):
        here = pl.ds(pl.multiple_of(k * part, part), part)
        value = sum(gain[t] * mains[t, here, :] for t in range(slots))
        terms[here, :] = jnp.where(core == 0, value[:, :lanes], value[:, lanes:])
        crossing[here, :] = jnp.where(core == 0, value[:, lanes:], value[:, :lanes]).astype(BF16)
        return carry

    order = far + [z]
    pairs = []
    for i, zd in enumerate(order):
        lax.fori_loop(zd * steps, (zd + 1) * steps, term, 0)
        span = pl.ds(pl.multiple_of(chunk * zd, 64), chunk)
        pairs.append(remote(crossing.at[span, :], pair_in.at[span, :], p_ss.at[i], p_rs.at[i], *sibling))
        pairs[i].start()

    def share(zd, dy, dx):
        row = chunk * zd + block * ((y + dy) % 2) + half * ((xc + dx) % 2)
        return pl.ds(pl.multiple_of(row, 16), half)

    shares = []
    for i, zd in enumerate(order):
        pairs[i].wait_recv()

        def add_pair(m, carry, zd=zd):
            here = pl.ds(pl.multiple_of(zd * chunk + m * part, part), part)
            summing = terms[here, :] + pair_in[here, :].astype(F32)
            terms[here, :] = summing
            summed[here, :] = summing.astype(BF16)
            return carry

        lax.fori_loop(0, steps, add_pair, 0)
        for m, (dy, dx) in enumerate(plane):
            copy = remote(
                summed.at[share(zd, dy, dx), :], rs_in.at[i, m], r_ss.at[3 * i + m], r_rs.at[3 * i + m], *at(0, dy, dx, 0)
            )
            copy.start()
            shares.append(copy)

    def rescale(t, carry):
        factor = facts[pl.ds(t, 1), :]
        for r in range(rows):
            for b in range(3):
                tap = slice(b * ch, (b + 1) * ch)
                scaled[t, r + 1, :, tap] = (gcat[t * rows + r, :, tap].astype(F32) * factor).astype(BF16)
        return carry

    w_cross(1)
    w_cross(0)
    lax.fori_loop(0, slots, rescale, 0)
    remote(other_block(1 - core), other_block(1 - core), sw_ss.at[zs - 1], sw_rs.at[z], *sibling).wait_recv()
    for j in (2, 1, 0):
        place = group(far[j], 1 - core)
        remote(place, place, sw_ss.at[j], sw_rs.at[far[j]], *sibling).wait_recv()

    def sums(k, dots):
        here = pl.ds(pl.multiple_of(k * part, part), part)
        wv = jnp.concatenate([wfull[0, here, :], wfull[1, here, :]], axis=1).astype(F32)
        return tuple(dots[t] + fold(wv * mains[t, here, :]) for t in range(slots))

    zero = jnp.zeros((8, ch), F32)
    dots = lax.fori_loop(0, 9 * ch // part, sums, (zero,) * slots)
    for t in range(slots):
        pull = live[t] * demod[t] * demod[t] * demod[t] * jnp.sum(dots[t], axis=0, keepdims=True) * scale
        pull_all[s, d, t : t + 1, :] = pull[:, :lanes]
        pull_all[s, d, slots + t : slots + t + 1, :] = pull[:, lanes:]
    spread(pull_all, pl_ss, pl_rs)

    for way, (_, _, takes) in enumerate(ways):
        @pl.when(takes)
        def _(way=way):
            halos[way][1].wait_recv()

    def edges():
        for t in range(slots):
            for b in range(3):
                tap = slice(b * ch, (b + 1) * ch)
                above, factor = (slots * rows, hdem_in[0, 0:1, :]) if t == 0 else (t * rows - 1, demod[t - 1])
                scaled[t, 0, :, tap] = (gcat[above, :, tap].astype(F32) * (factor * top_on[t])).astype(BF16)
                below = gcat[slots * rows + 1, :, tap].astype(F32) * (hdem_in[1, 0:1, :] * last_on[t])
                if t < slots - 1:
                    below = below + gcat[(t + 1) * rows, :, tap].astype(F32) * (demod[t + 1] * next_on[t])
                scaled[t, rows + 1, :, tap] = below.astype(BF16)
        for a in range(3):
            for b in range(3):
                tap = 3 * a + b
                for h in range(2):
                    wcat[a, :, b * ch + h * lanes : b * ch + (h + 1) * lanes] = wfull[h, tap * ch : (tap + 1) * ch, :]

    def tile_back(t, carry):
        found = None
        for a in range(3):
            left = scaled[t, 2 - a : 2 - a + rows].reshape(rows * cols, 3 * ch)
            more = lax.dot_general(left, wcat[a], (((1,), (1,)), ((), ())), preferred_element_type=F32)
            found = more if found is None else found + more
        found = (found * style_ref[pl.ds(t, 1), :]).astype(BF16)
        tg_ref[t] = found.reshape(rows, cols, ch)
        return carry

    edges()
    lines = []
    for i, zd in enumerate(order):
        own = terms[share(zd, 0, 0), :]
        for m in range(3):
            shares[3 * i + m].wait_recv()
            own = own + rs_in[i, m].astype(F32)
        if i < zs - 1:
            line_out[i] = own.astype(BF16)
            lines.append(remote(line_out.at[i], line_in.at[z], l_ss.at[i], l_rs.at[z], zd * 2 + y, s))
            lines[-1].start()
        if i == zs - 2:
            collect(pull_all, pl_ss, pl_rs)
            for k in range(1, secs):
                send(remote(pull_all.at[s], pull_all.at[s], px_ss.at[k - 1], px_rs.at[k - 1], d, (s + k) % secs))
        if i < zs - 1:
            lax.fori_loop(i * slots // zs, (i + 1) * slots // zs, tile_back, 0)
    lax.fori_loop((zs - 1) * slots // zs, slots, tile_back, 0)
    for j in (2, 1, 0):
        place = line_in.at[far[j]]
        remote(line_out.at[j], place, l_ss.at[j], l_rs.at[far[j]], far[j] * 2 + y, s).wait_recv()
        own = own + line_in[far[j]].astype(F32)
    fin[s] = own.astype(BF16)
    gathers = []
    for k in range(1, secs):
        copy = remote(fin.at[s], fin.at[s], a_ss.at[k - 1], a_rs.at[k - 1], d, (s + k) % secs)
        copy.start()
        gathers.append(copy)

    for k in range(1, secs):
        for ref, ss, rs in ((sq_all, sx_ss, sx_rs), (pull_all, px_ss, px_rs)):
            place = ref.at[(s + secs - k) % secs]
            remote(place, place, ss.at[k - 1], rs.at[k - 1], d, (s + k) % secs).wait_recv()
    tall = secs * wide
    upper = lax.broadcasted_iota(jnp.int32, (tall, lanes), 0) % (2 * slots) < slots

    def unpacked(ref):
        value = ref[...].reshape(tall, lanes)
        moved = pltpu.roll(value, tall - slots, 0)
        return jnp.concatenate([jnp.where(upper, value, 0.0), jnp.where(upper, moved, 0.0)], axis=1)

    coupled = jnp.dot(
        unpacked(sq_all).T, unpacked(pull_all), precision=lax.Precision.HIGHEST, preferred_element_type=F32
    )
    coup[0:ch, :] = coupled
    coup[ch : 2 * ch, :] = coupled
    for q in range(secs):
        row, h = half * (q // 2), q % 2
        w_own = wfull[h, pl.ds(pl.multiple_of(block * d + row, 16), half), :].astype(F32)
        c_own = coup[pl.ds(pl.multiple_of(shift + row, 16), half), h * lanes : (h + 1) * lanes]
        wg_ref[row : row + half, h * lanes : (h + 1) * lanes] = w_own * c_own
    for k in range(1, secs):
        other = fin.at[(s + secs - k) % secs]
        remote(other, other, a_ss.at[k - 1], a_rs.at[k - 1], d, (s + k) % secs).wait_recv()
    for q in range(secs):
        row, h = half * (q // 2), q % 2
        span = (slice(row, row + half), slice(h * lanes, (h + 1) * lanes))
        wg_ref[span] = fin[q].astype(F32) - wg_ref[span]
    for way, (_, gives, _) in enumerate(ways):
        @pl.when(gives)
        def _(way=way):
            for copy in halos[way]:
                copy.wait_send()

    for copy in sends + pairs + shares + lines + gathers:
        copy.wait_send()


def store_kernel(tg_ref, wg_ref, tg_out, wg_out, t_sem, w_sem):
    copies = [pltpu.make_async_copy(tg_ref.at[t], tg_out.at[t], t_sem.at[t]) for t in range(tg_ref.shape[0])]
    copies.append(pltpu.make_async_copy(wg_ref, wg_out, w_sem))
    for copy in copies:
        copy.start()
    for copy in copies:
        copy.wait()


def fused(dps, secs, tiles, out_grad, style, weight, tile_counts, crop_first):
    slots, rows, cols, ch = tiles.shape
    block = weight.shape[0]
    half = block // 2
    lanes = ch // 2
    zs = dps // 2
    scale = 1.0 / (slots * dps * secs * rows * cols) ** 0.5
    dma = pltpu.SemaphoreType.DMA
    vmem = pl.BlockSpec(memory_space=pltpu.VMEM)
    hbm = pl.BlockSpec(memory_space=pltpu.HBM)
    counts = [dps - 1, dps, secs - 1, secs - 1, dps - 1, dps, dps - 1, dps, secs - 1, secs - 1]
    counts += [zs - 1, zs, 1, 1, 3 * zs - 3, 3 * zs, zs, zs, zs, zs, 3 * zs, 3 * zs, zs - 1, zs, secs - 1, secs - 1]
    tg, wg = pl.pallas_call(
        functools.partial(fused_kernel, dps, secs, scale),
        out_shape=(
            pltpu.VMEM(tiles.shape, BF16),
            pltpu.VMEM(weight.shape, F32),
        ),
        in_specs=[hbm] * 6,
        out_specs=(vmem, vmem),
        scratch_shapes=[
            pltpu.SMEM(tile_counts.shape, jnp.int32),
            pltpu.SMEM(crop_first.shape, jnp.int32),
            pltpu.VMEM(tiles.shape, BF16),
            pltpu.VMEM(tiles.shape, BF16),
            pltpu.VMEM(style.shape, F32),
            pltpu.VMEM((2, 9 * ch, lanes), BF16),
            pltpu.VMEM((2, 2, cols, ch), BF16),
            pltpu.VMEM((2, 2, cols, ch), BF16),
            pltpu.VMEM((2, 8, ch), F32),
            pltpu.VMEM((2, 8, ch), F32),
            pltpu.VMEM((2 * ch, ch), F32),
            pltpu.VMEM((secs, dps, 2 * slots, lanes), F32),
            pltpu.VMEM((dps, 2 * slots, lanes), F32),
            pltpu.VMEM((dps, 2 * slots, lanes), F32),
            pltpu.VMEM((secs, dps, 2 * slots, lanes), F32),
            pltpu.VMEM((2 * ch, ch), F32),
            pltpu.VMEM((slots, ch, (rows + 2) * cols), BF16),
            pltpu.VMEM((slots * rows + 2, cols, 3 * ch), BF16),
            pltpu.VMEM((slots, 9 * ch, ch), F32),
            pltpu.VMEM((3, ch, 3 * ch), BF16),
            pltpu.VMEM((slots, rows + 2, cols, 3 * ch), BF16),
            pltpu.VMEM((8, ch), F32),
            pltpu.VMEM((9 * ch, lanes), F32),
            pltpu.VMEM((9 * ch, lanes), BF16),
            pltpu.VMEM((9 * ch, lanes), BF16),
            pltpu.VMEM((9 * ch, lanes), BF16),
            pltpu.VMEM((zs, 3, half, lanes), BF16),
            pltpu.VMEM((zs - 1, half, lanes), BF16),
            pltpu.VMEM((zs, half, lanes), BF16),
            pltpu.VMEM((secs, half, lanes), BF16),
            dma((7,)), dma((4,)), dma((4,)),
        ] + [dma((count,)) for count in counts],
        compiler_params=pltpu.CompilerParams(collective_id=0, has_side_effects=True, vmem_limit_bytes=56 * 1024 * 1024),
        name="fused_backward",
    )(tile_counts, crop_first, tiles, out_grad, style, weight)
    return pl.pallas_call(
        store_kernel,
        out_shape=(
            jax.ShapeDtypeStruct(tiles.shape, BF16),
            jax.ShapeDtypeStruct(weight.shape, F32),
        ),
        in_specs=[vmem, vmem],
        out_specs=(hbm, hbm),
        scratch_shapes=[dma((slots,)), dma],
        compiler_params=pltpu.CompilerParams(has_side_effects=True, vmem_limit_bytes=1024 * 1024),
        name="store_out",
    )(tg, wg)


def solution(mesh):
    placed = (
        P(("dp", "section"), None, None, None),
        P(("dp", "section"), None, None, None),
        P(("dp", "section"), None),
        P("dp", None),
        P(("dp", "section")),
        P(("dp", "section")),
    )
    dps, secs = mesh.shape["dp"], mesh.shape["section"]

    def body(tiles, out_grad, style, weight, tile_counts, crop_first):
        args = (tiles, out_grad, style, weight, tile_counts, crop_first)
        rows, ch = weight.shape
        if secs == 4 and dps == 8 and tiles.shape[0] == 4 and rows % 32 == 0 and ch <= rows < 2 * ch:
            return fused(dps, secs, *args)
        return per_device(*args)

    return jax.shard_map(
        body,
        mesh=mesh,
        in_specs=placed,
        out_specs=(P(("dp", "section"), None, None, None), P("dp", None)),
        check_vma=False,
    )
```

```python
import functools

import jax
import jax.numpy as jnp
from jax import lax
from jax.experimental import pallas as pl
from jax.experimental.pallas import tpu as pltpu
from jax.sharding import PartitionSpec as P


def from_behind(value, axis, steps):
    count = lax.axis_size(axis)
    leading, last = (max(0, -steps), min(count, count - steps))
    return lax.ppermute(value, axis, [(source, source + steps) for source in range(leading, last)])


def tile_block(modulated, scaled, out_grad, style, live, demod, top, bottom, w_taps):
    rows = modulated.shape[1]
    cols = modulated.shape[2]
    ext_mod = jnp.concatenate([top[:, 0][:, None], modulated, bottom[:, 0][:, None]], axis=1)
    ext_grad = jnp.concatenate([top[:, 1][:, None], scaled, bottom[:, 1][:, None]], axis=1)
    pad_mod = jnp.pad(ext_mod, ((0, 0), (0, 0), (1, 1), (0, 0)))
    pad_grad = jnp.pad(ext_grad, ((0, 0), (0, 0), (1, 1), (0, 0)))
    raw_out = jnp.zeros(out_grad.shape, jnp.float32)
    grad_in = jnp.zeros(modulated.shape, jnp.float32)
    mains = []
    for row_off in range(3):
        for col_off in range(3):
            tap = row_off * 3 + col_off
            window = pad_mod[:, row_off : row_off + rows, col_off : col_off + cols, :]
            raw_out = raw_out + jnp.einsum(
                "trpi,io->trpo", window, w_taps[tap], preferred_element_type=jnp.float32
            )
            back = pad_grad[
                :, 2 - row_off : 2 - row_off + rows, 2 - col_off : 2 - col_off + cols, :
            ]
            grad_in = grad_in + jnp.einsum(
                "trpo,io->trpi", back, w_taps[tap], preferred_element_type=jnp.float32
            )
            mains.append(
                jnp.einsum("trpi,trpo->io", window, scaled, preferred_element_type=jnp.float32)
            )
    tile_grad = (grad_in * style[:, None, None, :]).astype(jnp.bfloat16)
    demod_dot = (
        live[:, None] * demod**3 * jnp.sum(out_grad.astype(jnp.float32) * raw_out, axis=(1, 2))
    )
    coupling = jnp.dot((style * style).T, demod_dot, precision=lax.Precision.HIGHEST)
    term = jnp.stack(mains) - w_taps.astype(jnp.float32) * coupling[None]
    return (tile_grad, term)


def per_device(tiles, out_grad, style, weight, tile_counts, crop_first):
    channels = weight.shape[1]
    slot_count = tiles.shape[0]
    devices = lax.axis_size("dp") * lax.axis_size("section")
    scale = 1.0 / (slot_count * devices * tiles.shape[1] * tiles.shape[2]) ** 0.5
    full_weight = lax.all_gather(weight, "dp", axis=0, tiled=True)
    w_taps = full_weight.reshape(9, channels, channels)
    w_float = w_taps.astype(jnp.float32)
    w_square = jnp.sum(w_float * w_float, axis=0)
    count = tile_counts[0]
    slot_ids = jnp.arange(slot_count, dtype=jnp.int32)
    live = (slot_ids < count).astype(jnp.float32)
    demod = lax.rsqrt(jnp.dot(style * style, w_square, precision=lax.Precision.HIGHEST) + 1e-08)
    modulated = (tiles.astype(jnp.float32) * style[:, None, None, :]).astype(jnp.bfloat16)
    scaled = (
        out_grad.astype(jnp.float32) * demod[:, None, None, :] * live[:, None, None, None]
    ).astype(jnp.bfloat16)
    edge = jnp.stack([modulated[:, -1], scaled[:, -1]], axis=1)
    head = jnp.stack([modulated[:, 0], scaled[:, 0]], axis=1)
    last_live = lax.dynamic_index_in_dim(edge, count - 1, 0, keepdims=False)
    recv_top = from_behind(last_live, ("dp", "section"), 1)
    first_sent = head[0] * (1 - crop_first[0]).astype(jnp.bfloat16)
    recv_bot = from_behind(first_sent, ("dp", "section"), -1)
    zero_slot = jnp.zeros((1,) + edge.shape[1:], jnp.bfloat16)
    top_local = jnp.concatenate([zero_slot, edge[:-1]], axis=0)
    top_mask = ((live > 0) & (crop_first == 0)).astype(jnp.bfloat16)
    top = (
        jnp.where((slot_ids == 0)[:, None, None, None], recv_top[None], top_local)
        * top_mask[:, None, None, None]
    )
    next_link = jnp.concatenate(
        [live[1:] * (1 - crop_first[1:]).astype(jnp.float32), jnp.zeros((1,), jnp.float32)], axis=0
    )
    bot_local = (
        jnp.concatenate([head[1:], zero_slot], axis=0)
        * next_link.astype(jnp.bfloat16)[:, None, None, None]
    )
    bottom = jnp.where((slot_ids == count - 1)[:, None, None, None], recv_bot[None], bot_local)
    tile_grad, term = tile_block(
        modulated, scaled, out_grad, style, live, demod, top, bottom, w_taps
    )
    flat_term = (term * scale).reshape(9 * channels, channels)
    shard = lax.psum_scatter(flat_term, "dp", scatter_dimension=0, tiled=True)
    weight_grad = lax.psum(shard, "section")
    return (tile_grad, weight_grad)


MESH = pl.DeviceIdType.MESH
F32 = jnp.float32
BF16 = jnp.bfloat16


def rolled(value, steps):
    wide = value.shape[0]
    place = lax.broadcasted_iota(jnp.int32, value.shape, 0)
    moved = pltpu.roll(value, steps % wide, 0)
    keep = (place >= steps) if steps > 0 else (place < wide + steps)
    return jnp.where(keep, moved, 0.0)


def fold(value):
    return value.reshape(value.shape[0] // 8, 8, value.shape[1]).sum(axis=0)


def fused_kernel(
    dps, secs, scale,
    count_hbm, first_hbm, tiles_hbm, g_hbm, style_hbm, w_hbm,
    tg_ref, wg_ref,
    count_ref, first_ref, tiles_ref, g_ref, style_ref, wfull, halo_out, halo_in, hdem_out, hdem_in, wsq, sq_all, norm_out, norm_in,
    pull_all, coup, modt, gcat, mains, wcat, scaled, facts, terms, crossing, pair_in, summed, rs_in,
    line_out, line_in, zin, fin,
    in_sem, h_ss, h_rs, sq_ss, sq_rs, sx_ss, sx_rs, nm_ss, nm_rs, pl_ss, pl_rs, px_ss, px_rs,
    wz_ss, wz_rs, wo_ss, wo_rs, wp_ss, wp_rs, sw_ss, sw_rs, p_ss, p_rs, r_ss, r_rs, l_ss, l_rs, zn_ss, zn_rs, a_ss, a_rs,
):
    slots, rows, cols, ch = tiles_ref.shape
    block = w_hbm.shape[0]
    half = block // 2
    lanes = ch // 2
    d = lax.axis_index("dp")
    s = lax.axis_index("section")
    n = d * secs + s
    total = dps * secs
    core = s % 2
    xc = s // 2
    zs = dps // 2
    z = d // 2
    y = d % 2

    def remote(src, dst, ss, rs, dp, sec):
        return pltpu.make_async_remote_copy(
            src_ref=src, dst_ref=dst, send_sem=ss, recv_sem=rs,
            device_id=(dp, sec), device_id_type=MESH,
        )

    def at(dz, dy, dx, dc):
        return ((z + dz) % zs) * 2 + (y + dy) % 2, ((xc + dx) % 2) * 2 + (core + dc) % 2

    after, before = (n + 1) % total, (n + total - 1) % total
    plane = ((1, 1), (1, 0), (0, 1))
    sibling = at(0, 0, 0, 1)
    other_y = at(0, 1, 0, 0)
    far = [3 - 3 * (z // 2), 2 - z // 2, z + 1 - 2 * (z % 2)]
    barrier = pltpu.get_barrier_semaphore()
    others = [far[j] * 2 + (y + dy) % 2 for j in range(zs - 1) for dy in (1, 0)] + [z * 2 + 1 - y]
    peers = [(owner, s) for owner in others] + [(d, (s + k) % secs) for k in range(1, secs)]
    peers += [at(0, 1, 1, 0), (after // secs, after % secs), (before // secs, before % secs)]
    for peer in peers:
        pl.semaphore_signal(barrier, inc=1, device_id=peer, device_id_type=MESH)

    mine = pl.ds(pl.multiple_of(block * d, 16), block)
    loads = [
        pltpu.make_async_copy(style_hbm, style_ref, in_sem.at[0]),
        pltpu.make_async_copy(w_hbm.at[:, 0:lanes], wfull.at[0, mine, :], in_sem.at[1]),
        pltpu.make_async_copy(w_hbm.at[:, lanes:ch], wfull.at[1, mine, :], in_sem.at[2]),
        pltpu.make_async_copy(tiles_hbm, tiles_ref, in_sem.at[3]),
        pltpu.make_async_copy(g_hbm, g_ref, in_sem.at[4]),
        pltpu.make_async_copy(count_hbm, count_ref, in_sem.at[5]),
        pltpu.make_async_copy(first_hbm, first_ref, in_sem.at[6]),
    ]
    for load in loads:
        load.start()
    sends = []

    def send(copy):
        copy.start()
        sends.append(copy)

    loads[0].wait()
    square = style_ref[...] * style_ref[...]
    sq_all[s, d, 0:slots, :] = square[:, :lanes]
    sq_all[s, d, slots : 2 * slots, :] = square[:, lanes:]
    pl.semaphore_wait(barrier, len(peers))

    def spread(ref, ss, rs):
        for i, owner in enumerate(others):
            send(remote(ref.at[s, d], ref.at[s, d], ss.at[i], rs.at[d], owner, s))

    def collect(ref, ss, rs):
        for i, owner in enumerate(others):
            remote(ref.at[s, owner], ref.at[s, owner], ss.at[i], rs.at[owner], owner, s).wait_recv()

    spread(sq_all, sq_ss, sq_rs)
    loads[3].wait()
    loads[4].wait()
    loads[5].wait()
    loads[6].wait()
    count = count_ref[0]
    row_t = tiles_ref[0, rows - 1].astype(F32)
    row_g = g_ref[0, rows - 1].astype(F32)
    row_s = style_ref[0:1, :]
    for t in range(1, slots):
        here = count - 1 == t
        row_t = jnp.where(here, tiles_ref[t, rows - 1].astype(F32), row_t)
        row_g = jnp.where(here, g_ref[t, rows - 1].astype(F32), row_g)
        row_s = jnp.where(here, style_ref[t : t + 1, :], row_s)
    halo_out[0, 0] = (row_t * row_s).astype(BF16)
    halo_out[0, 1] = row_g.astype(BF16)
    open_first = (1 - first_ref[0]).astype(F32)
    halo_out[1, 0] = (tiles_ref[0, 0].astype(F32) * style_ref[0:1, :] * open_first).astype(BF16)
    halo_out[1, 1] = (g_ref[0, 0].astype(F32) * open_first).astype(BF16)
    ways = ((after, n < total - 1, n > 0), (before, n > 0, n < total - 1))
    halos = []
    for way, (to, _, _) in enumerate(ways):
        halos.append([
            remote(halo_out.at[way], halo_in.at[way], h_ss.at[way], h_rs.at[way], to // secs, to % secs),
            remote(hdem_out.at[way], hdem_in.at[way], h_ss.at[2 + way], h_rs.at[2 + way], to // secs, to % secs),
        ])
    for way, (_, gives, takes) in enumerate(ways):
        @pl.when(gives)
        def _(way=way):
            halos[way][0].start()

        @pl.when(jnp.logical_not(takes))
        def _(way=way):
            halo_in[way] = jnp.zeros_like(halo_in[way])
            hdem_in[way] = jnp.zeros_like(hdem_in[way])

    loads[1].wait()
    loads[2].wait()

    def w_part(owner, which):
        return wfull.at[core, pl.ds(pl.multiple_of(block * owner + half * which, 16), half), :]

    for j in (2, 1, 0):
        send(remote(w_part(d, xc), w_part(d, xc), wz_ss.at[j], wz_rs.at[z], far[j] * 2 + y, s))
    own_w = wfull.at[core, mine, :]
    send(remote(own_w, own_w, wo_ss.at[0], wo_rs.at[0], *other_y))

    for h in range(2):
        w_own = wfull[h, mine, :].astype(F32)
        w_own = w_own * w_own
        folded = jnp.concatenate([w_own[: block - ch] + w_own[ch:], w_own[block - ch : ch]], axis=0)
        wsq[0:ch, h * lanes : (h + 1) * lanes] = folded
        wsq[ch : 2 * ch, h * lanes : (h + 1) * lanes] = folded
    shift = (block * d) % ch

    def put_g(row, value):
        gcat[row, :, 0:ch] = rolled(value, -1).astype(BF16)
        gcat[row, :, ch : 2 * ch] = value.astype(BF16)
        gcat[row, :, 2 * ch : 3 * ch] = rolled(value, 1).astype(BF16)

    def prepare(t, carry):
        row_style = style_ref[pl.ds(t, 1), :]
        for r in range(rows):
            value = (tiles_ref[t, r].astype(F32) * row_style).astype(BF16)
            modt[t, :, (r + 1) * cols : (r + 2) * cols] = value.T
            put_g(t * rows + r, g_ref[t, r].astype(F32))
        return carry

    lax.fori_loop(0, slots, prepare, 0)

    live = [(t < count).astype(F32) for t in range(slots)]
    shut = [(first_ref[t] == 0).astype(F32) for t in range(slots)]
    top_on = [live[t] * shut[t] for t in range(slots)]
    top_on[0] = top_on[0] * (n > 0).astype(F32)
    next_on = [live[t + 1] * shut[t + 1] for t in range(slots - 1)]
    last_on = [(count - 1 == t).astype(F32) * (n < total - 1).astype(F32) for t in range(slots)]

    def tile_mains(taps, t, carry):
        right = gcat[pl.ds(t * rows, rows)].reshape(rows * cols, 3 * ch)
        for a in taps:
            found = jnp.dot(modt[t, :, a * cols : (a + rows) * cols], right, preferred_element_type=F32)
            for b in range(3):
                tap = 3 * a + b
                mains[t, tap * ch : (tap + 1) * ch, :] = found[:, b * ch : (b + 1) * ch]
        return carry

    lax.fori_loop(0, slots, functools.partial(tile_mains, (1,)), 0)

    def w_forward(j):
        place = w_part(far[j] * 2 + y, xc)
        remote(place, place, wz_ss.at[j], wz_rs.at[far[j]], far[j] * 2 + y, s).wait_recv()
        for m, (dy, dx) in enumerate(plane):
            send(remote(place, place, wp_ss.at[3 * j + m], wp_rs.at[3 * far[j] + m], *at(0, dy, dx, 0)))

    w_forward(2)
    collect(sq_all, sq_ss, sq_rs)
    wide = dps * 2 * slots
    squares = sq_all[s].reshape(wide, lanes)
    aligned = wsq[pl.ds(pl.multiple_of(ch - shift, 16), ch), :]
    low = jnp.dot(squares, aligned[:lanes], precision=lax.Precision.HIGHEST, preferred_element_type=F32)
    high = jnp.dot(squares, aligned[lanes:], precision=lax.Precision.HIGHEST, preferred_element_type=F32)
    both = low + pltpu.roll(high, wide - slots, 0)
    upper = lax.broadcasted_iota(jnp.int32, (wide, lanes), 0) % (2 * slots) < slots
    packed = jnp.where(upper, both[:, :lanes], pltpu.roll(both[:, lanes:], slots, 0))
    norm_out[...] = packed.reshape(dps, 2 * slots, lanes)
    for i, owner in enumerate(others):
        send(remote(norm_out.at[owner], norm_in.at[d], nm_ss.at[i], nm_rs.at[d], owner, s))
    norm_in[d] = norm_out[d]
    for k in range(1, secs):
        send(remote(sq_all.at[s], sq_all.at[s], sx_ss.at[k - 1], sx_rs.at[k - 1], d, (s + k) % secs))

    w_forward(1)
    for way, (_, _, takes) in enumerate(ways):
        @pl.when(takes)
        def _(way=way):
            halos[way][0].wait_recv()

    put_g(slots * rows, halo_in[0, 1].astype(F32))
    put_g(slots * rows + 1, halo_in[1, 1].astype(F32))
    from_prev = halo_in[0, 0].T.astype(F32)
    from_next = halo_in[1, 0].T.astype(F32)
    for t in range(slots):
        above = from_prev if t == 0 else modt[t - 1, :, rows * cols : (rows + 1) * cols].astype(F32)
        modt[t, :, 0:cols] = (above * top_on[t]).astype(BF16)
        below = from_next * last_on[t]
        if t < slots - 1:
            below = below + modt[t + 1, :, cols : 2 * cols].astype(F32) * next_on[t]
        modt[t, :, (rows + 1) * cols : (rows + 2) * cols] = below.astype(BF16)

    lax.fori_loop(0, 1, functools.partial(tile_mains, (0, 2)), 0)
    w_forward(0)
    lax.fori_loop(1, slots, functools.partial(tile_mains, (0, 2)), 0)

    chunk = 2 * block

    def group(zd, which):
        return wfull.at[which, pl.ds(pl.multiple_of(chunk * zd, 16), chunk), :]

    def other_block(which):
        return wfull.at[which, pl.ds(pl.multiple_of(block * (2 * z + 1 - y), 16), block), :]

    def w_cross(j):
        for m, (dy, dx) in enumerate(plane):
            place = w_part(far[j] * 2 + (y + dy) % 2, (xc + dx) % 2)
            remote(place, place, wp_ss.at[3 * j + m], wp_rs.at[3 * far[j] + m], *at(0, dy, dx, 0)).wait_recv()
        send(remote(group(far[j], core), group(far[j], core), sw_ss.at[j], sw_rs.at[far[j]], *sibling))

    remote(other_block(core), other_block(core), wo_ss.at[0], wo_rs.at[0], *other_y).wait_recv()
    send(remote(other_block(core), other_block(core), sw_ss.at[zs - 1], sw_rs.at[z], *sibling))
    w_cross(2)
    for i, owner in enumerate(others):
        remote(norm_out.at[owner], norm_in.at[owner], nm_ss.at[i], nm_rs.at[owner], owner, s).wait_recv()
    inverse = lax.rsqrt(norm_in[...].sum(axis=0) + 1e-08)
    demod = [
        jnp.concatenate([inverse[t : t + 1, :], inverse[slots + t : slots + t + 1, :]], axis=1)
        for t in range(slots)
    ]
    gain = [demod[t] * live[t] * scale for t in range(slots)]
    for t in range(slots):
        facts[t : t + 1, :] = demod[t] * live[t]

    last = demod[0]
    for t in range(1, slots):
        last = jnp.where(count - 1 == t, demod[t], last)
    hdem_out[0] = jnp.broadcast_to(last, (8, ch))
    hdem_out[1] = jnp.broadcast_to(demod[0], (8, ch))
    for way, (_, gives, _) in enumerate(ways):
        @pl.when(gives)
        def _(way=way):
            halos[way][1].start()

    part = 64
    steps = chunk // part

    def term(k, carry):
        here = pl.ds(pl.multiple_of(k * part, part), part)
        value = sum(gain[t] * mains[t, here, :] for t in range(slots))
        terms[here, :] = jnp.where(core == 0, value[:, :lanes], value[:, lanes:])
        crossing[here, :] = jnp.where(core == 0, value[:, lanes:], value[:, :lanes]).astype(BF16)
        return carry

    order = [far[2], far[0], far[1], z]
    pairs = []
    for i, zd in enumerate(order):
        lax.fori_loop(zd * steps, (zd + 1) * steps, term, 0)
        span = pl.ds(pl.multiple_of(chunk * zd, 64), chunk)
        pairs.append(remote(crossing.at[span, :], pair_in.at[span, :], p_ss.at[i], p_rs.at[i], *sibling))
        pairs[i].start()

    def share(zd, dy, dx, low=0):
        row = chunk * zd + block * ((y + dy) % 2) + half * ((xc + dx) % 2) + low
        return pl.ds(pl.multiple_of(row, 16), half - low)

    shares = []

    def plane_send(i, zd, low=0):
        size = half - low
        for m, (dy, dx) in enumerate(plane):
            copy = remote(
                summed.at[share(zd, dy, dx, low), :], rs_in.at[i, m, 0:size, :], r_ss.at[3 * i + m], r_rs.at[3 * i + m],
                *at(0, dy, dx, 0)
            )
            copy.start()
            shares.append(copy)

    early = half * 5 // 9 // 16 * 16
    hops = []
    for q in range(4):
        source = summed.at[pl.ds(pl.multiple_of(chunk * far[2] + half * q, 16), early), :]
        place = zin.at[half * q : half * q + early, :]
        hops.append(remote(source, place, zn_ss.at[q], zn_rs.at[q], far[2] * 2 + y, s))
    for i, zd in enumerate(order):
        pairs[i].wait_recv()

        def add_pair(m, carry, zd=zd):
            here = pl.ds(pl.multiple_of(zd * chunk + m * part, part), part)
            summing = terms[here, :] + pair_in[here, :].astype(F32)
            terms[here, :] = summing
            summed[here, :] = summing.astype(BF16)
            return carry

        lax.fori_loop(0, steps, add_pair, 0)
        if i == 0:
            for hop in hops:
                send(hop)
        elif i < zs - 1:
            plane_send(i - 1, zd)
    plane_send(zs - 2, far[2], early)

    def rescale(t, carry):
        factor = facts[pl.ds(t, 1), :]
        for r in range(rows):
            for b in range(3):
                tap = slice(b * ch, (b + 1) * ch)
                scaled[t, r + 1, :, tap] = (gcat[t * rows + r, :, tap].astype(F32) * factor).astype(BF16)
        return carry

    w_cross(1)
    w_cross(0)
    lax.fori_loop(0, slots, rescale, 0)
    remote(other_block(1 - core), other_block(1 - core), sw_ss.at[zs - 1], sw_rs.at[z], *sibling).wait_recv()
    for j in (2, 1, 0):
        place = group(far[j], 1 - core)
        remote(place, place, sw_ss.at[j], sw_rs.at[far[j]], *sibling).wait_recv()

    def sums(k, dots):
        here = pl.ds(pl.multiple_of(k * part, part), part)
        wv = jnp.concatenate([wfull[0, here, :], wfull[1, here, :]], axis=1).astype(F32)
        return tuple(dots[t] + fold(wv * mains[t, here, :]) for t in range(slots))

    zero = jnp.zeros((8, ch), F32)
    dots = lax.fori_loop(0, 9 * ch // part, sums, (zero,) * slots)
    for t in range(slots):
        pull = live[t] * demod[t] * demod[t] * demod[t] * jnp.sum(dots[t], axis=0, keepdims=True) * scale
        pull_all[s, d, t : t + 1, :] = pull[:, :lanes]
        pull_all[s, d, slots + t : slots + t + 1, :] = pull[:, lanes:]
    spread(pull_all, pl_ss, pl_rs)

    for way, (_, _, takes) in enumerate(ways):
        @pl.when(takes)
        def _(way=way):
            halos[way][1].wait_recv()

    def edges():
        for t in range(slots):
            for b in range(3):
                tap = slice(b * ch, (b + 1) * ch)
                above, factor = (slots * rows, hdem_in[0, 0:1, :]) if t == 0 else (t * rows - 1, demod[t - 1])
                scaled[t, 0, :, tap] = (gcat[above, :, tap].astype(F32) * (factor * top_on[t])).astype(BF16)
                below = gcat[slots * rows + 1, :, tap].astype(F32) * (hdem_in[1, 0:1, :] * last_on[t])
                if t < slots - 1:
                    below = below + gcat[(t + 1) * rows, :, tap].astype(F32) * (demod[t + 1] * next_on[t])
                scaled[t, rows + 1, :, tap] = below.astype(BF16)
        for a in range(3):
            for b in range(3):
                tap = 3 * a + b
                for h in range(2):
                    wcat[a, :, b * ch + h * lanes : b * ch + (h + 1) * lanes] = wfull[h, tap * ch : (tap + 1) * ch, :]

    def tile_back(t, carry):
        found = None
        for a in range(3):
            left = scaled[t, 2 - a : 2 - a + rows].reshape(rows * cols, 3 * ch)
            more = lax.dot_general(left, wcat[a], (((1,), (1,)), ((), ())), preferred_element_type=F32)
            found = more if found is None else found + more
        found = (found * style_ref[pl.ds(t, 1), :]).astype(BF16)
        tg_ref[t] = found.reshape(rows, cols, ch)
        return carry

    for q, hop in enumerate(hops):
        hop.wait_recv()
        here = pl.ds(pl.multiple_of(chunk * z + half * q, 16), early)
        summing = terms[here, :] + zin[half * q : half * q + early, :].astype(F32)
        terms[here, :] = summing
        summed[here, :] = summing.astype(BF16)
    plane_send(zs - 1, z)
    edges()
    lines = []
    for i, zd in enumerate(order[1:-1] + [far[2], z]):
        low = early if i == zs - 2 else 0
        size = half - low
        own = terms[share(zd, 0, 0, low), :]
        for m in range(3):
            shares[3 * i + m].wait_recv()
            own = own + rs_in[i, m, 0:size, :].astype(F32)
        if i < zs - 1:
            line_out[i, 0:size, :] = own.astype(BF16)
            place = line_in.at[z, 0:size, :]
            lines.append(remote(line_out.at[i, 0:size, :], place, l_ss.at[i], l_rs.at[z], zd * 2 + y, s))
            lines[-1].start()
        if i == zs - 2:
            lax.fori_loop(0, slots - 2, tile_back, 0)
            collect(pull_all, pl_ss, pl_rs)
            for k in range(1, secs):
                send(remote(pull_all.at[s], pull_all.at[s], px_ss.at[k - 1], px_rs.at[k - 1], d, (s + k) % secs))
            lax.fori_loop(slots - 2, slots, tile_back, 0)
    for j in (2, 1, 0):
        size = half - early if j == 2 else half
        place = line_in.at[far[j], 0:size, :]
        remote(line_out.at[j, 0:size, :], place, l_ss.at[j], l_rs.at[far[j]], far[j] * 2 + y, s).wait_recv()
        more = line_in[far[j], 0:size, :].astype(F32)
        own = jnp.concatenate([own[:early], own[early:] + more], axis=0) if j == 2 else own + more
    fin[s] = own.astype(BF16)
    gathers = []
    for k in range(1, secs):
        copy = remote(fin.at[s], fin.at[s], a_ss.at[k - 1], a_rs.at[k - 1], d, (s + k) % secs)
        copy.start()
        gathers.append(copy)

    for k in range(1, secs):
        for ref, ss, rs in ((sq_all, sx_ss, sx_rs), (pull_all, px_ss, px_rs)):
            place = ref.at[(s + secs - k) % secs]
            remote(place, place, ss.at[k - 1], rs.at[k - 1], d, (s + k) % secs).wait_recv()
    tall = secs * wide
    upper = lax.broadcasted_iota(jnp.int32, (tall, lanes), 0) % (2 * slots) < slots

    def unpacked(ref):
        value = ref[...].reshape(tall, lanes)
        moved = pltpu.roll(value, tall - slots, 0)
        return jnp.concatenate([jnp.where(upper, value, 0.0), jnp.where(upper, moved, 0.0)], axis=1)

    coupled = jnp.dot(
        unpacked(sq_all).T, unpacked(pull_all), precision=lax.Precision.HIGHEST, preferred_element_type=F32
    )
    coup[0:ch, :] = coupled
    coup[ch : 2 * ch, :] = coupled
    for q in range(secs):
        row, h = half * (q // 2), q % 2
        w_own = wfull[h, pl.ds(pl.multiple_of(block * d + row, 16), half), :].astype(F32)
        c_own = coup[pl.ds(pl.multiple_of(shift + row, 16), half), h * lanes : (h + 1) * lanes]
        wg_ref[row : row + half, h * lanes : (h + 1) * lanes] = w_own * c_own
    for k in range(1, secs):
        other = fin.at[(s + secs - k) % secs]
        remote(other, other, a_ss.at[k - 1], a_rs.at[k - 1], d, (s + k) % secs).wait_recv()
    for q in range(secs):
        row, h = half * (q // 2), q % 2
        span = (slice(row, row + half), slice(h * lanes, (h + 1) * lanes))
        wg_ref[span] = fin[q].astype(F32) - wg_ref[span]
    for way, (_, gives, _) in enumerate(ways):
        @pl.when(gives)
        def _(way=way):
            for copy in halos[way]:
                copy.wait_send()

    for copy in sends + pairs + shares + lines + gathers:
        copy.wait_send()


def store_kernel(tg_ref, wg_ref, tg_out, wg_out, t_sem, w_sem):
    copies = [pltpu.make_async_copy(tg_ref.at[t], tg_out.at[t], t_sem.at[t]) for t in range(tg_ref.shape[0])]
    copies.append(pltpu.make_async_copy(wg_ref, wg_out, w_sem))
    for copy in copies:
        copy.start()
    for copy in copies:
        copy.wait()


def fused(dps, secs, tiles, out_grad, style, weight, tile_counts, crop_first):
    slots, rows, cols, ch = tiles.shape
    block = weight.shape[0]
    half = block // 2
    lanes = ch // 2
    zs = dps // 2
    scale = 1.0 / (slots * dps * secs * rows * cols) ** 0.5
    dma = pltpu.SemaphoreType.DMA
    vmem = pl.BlockSpec(memory_space=pltpu.VMEM)
    hbm = pl.BlockSpec(memory_space=pltpu.HBM)
    counts = [dps - 1, dps, secs - 1, secs - 1, dps - 1, dps, dps - 1, dps, secs - 1, secs - 1]
    counts += [zs - 1, zs, 1, 1, 3 * zs - 3, 3 * zs, zs, zs, zs, zs, 3 * zs, 3 * zs, zs - 1, zs, 4, 4, secs - 1, secs - 1]
    tg, wg = pl.pallas_call(
        functools.partial(fused_kernel, dps, secs, scale),
        out_shape=(
            pltpu.VMEM(tiles.shape, BF16),
            pltpu.VMEM(weight.shape, F32),
        ),
        in_specs=[hbm] * 6,
        out_specs=(vmem, vmem),
        scratch_shapes=[
            pltpu.SMEM(tile_counts.shape, jnp.int32),
            pltpu.SMEM(crop_first.shape, jnp.int32),
            pltpu.VMEM(tiles.shape, BF16),
            pltpu.VMEM(tiles.shape, BF16),
            pltpu.VMEM(style.shape, F32),
            pltpu.VMEM((2, 9 * ch, lanes), BF16),
            pltpu.VMEM((2, 2, cols, ch), BF16),
            pltpu.VMEM((2, 2, cols, ch), BF16),
            pltpu.VMEM((2, 8, ch), F32),
            pltpu.VMEM((2, 8, ch), F32),
            pltpu.VMEM((2 * ch, ch), F32),
            pltpu.VMEM((secs, dps, 2 * slots, lanes), F32),
            pltpu.VMEM((dps, 2 * slots, lanes), F32),
            pltpu.VMEM((dps, 2 * slots, lanes), F32),
            pltpu.VMEM((secs, dps, 2 * slots, lanes), F32),
            pltpu.VMEM((2 * ch, ch), F32),
            pltpu.VMEM((slots, ch, (rows + 2) * cols), BF16),
            pltpu.VMEM((slots * rows + 2, cols, 3 * ch), BF16),
            pltpu.VMEM((slots, 9 * ch, ch), F32),
            pltpu.VMEM((3, ch, 3 * ch), BF16),
            pltpu.VMEM((slots, rows + 2, cols, 3 * ch), BF16),
            pltpu.VMEM((8, ch), F32),
            pltpu.VMEM((9 * ch, lanes), F32),
            pltpu.VMEM((9 * ch, lanes), BF16),
            pltpu.VMEM((9 * ch, lanes), BF16),
            pltpu.VMEM((9 * ch, lanes), BF16),
            pltpu.VMEM((zs, 3, half, lanes), BF16),
            pltpu.VMEM((zs - 1, half, lanes), BF16),
            pltpu.VMEM((zs, half, lanes), BF16),
            pltpu.VMEM((2 * block, lanes), BF16),
            pltpu.VMEM((secs, half, lanes), BF16),
            dma((7,)), dma((4,)), dma((4,)),
        ] + [dma((count,)) for count in counts],
        compiler_params=pltpu.CompilerParams(collective_id=0, has_side_effects=True, vmem_limit_bytes=56 * 1024 * 1024),
        name="fused_backward",
    )(tile_counts, crop_first, tiles, out_grad, style, weight)
    return pl.pallas_call(
        store_kernel,
        out_shape=(
            jax.ShapeDtypeStruct(tiles.shape, BF16),
            jax.ShapeDtypeStruct(weight.shape, F32),
        ),
        in_specs=[vmem, vmem],
        out_specs=(hbm, hbm),
        scratch_shapes=[dma((slots,)), dma],
        compiler_params=pltpu.CompilerParams(has_side_effects=True, vmem_limit_bytes=1024 * 1024),
        name="store_out",
    )(tg, wg)


def solution(mesh):
    placed = (
        P(("dp", "section"), None, None, None),
        P(("dp", "section"), None, None, None),
        P(("dp", "section"), None),
        P("dp", None),
        P(("dp", "section")),
        P(("dp", "section")),
    )
    dps, secs = mesh.shape["dp"], mesh.shape["section"]

    def body(tiles, out_grad, style, weight, tile_counts, crop_first):
        args = (tiles, out_grad, style, weight, tile_counts, crop_first)
        rows, ch = weight.shape
        if secs == 4 and dps == 8 and tiles.shape[0] == 4 and rows % 32 == 0 and ch <= rows < 2 * ch:
            return fused(dps, secs, *args)
        return per_device(*args)

    return jax.shard_map(
        body,
        mesh=mesh,
        in_specs=placed,
        out_specs=(P(("dp", "section"), None, None, None), P("dp", None)),
        check_vma=False,
    )
```

```python
import functools

import jax
import jax.numpy as jnp
from jax import lax
from jax.experimental import pallas as pl
from jax.experimental.pallas import tpu as pltpu
from jax.sharding import PartitionSpec as P


def from_behind(value, axis, steps):
    count = lax.axis_size(axis)
    leading, last = (max(0, -steps), min(count, count - steps))
    return lax.ppermute(value, axis, [(source, source + steps) for source in range(leading, last)])


def tile_block(modulated, scaled, out_grad, style, live, demod, top, bottom, w_taps):
    rows = modulated.shape[1]
    cols = modulated.shape[2]
    ext_mod = jnp.concatenate([top[:, 0][:, None], modulated, bottom[:, 0][:, None]], axis=1)
    ext_grad = jnp.concatenate([top[:, 1][:, None], scaled, bottom[:, 1][:, None]], axis=1)
    pad_mod = jnp.pad(ext_mod, ((0, 0), (0, 0), (1, 1), (0, 0)))
    pad_grad = jnp.pad(ext_grad, ((0, 0), (0, 0), (1, 1), (0, 0)))
    raw_out = jnp.zeros(out_grad.shape, jnp.float32)
    grad_in = jnp.zeros(modulated.shape, jnp.float32)
    mains = []
    for row_off in range(3):
        for col_off in range(3):
            tap = row_off * 3 + col_off
            window = pad_mod[:, row_off : row_off + rows, col_off : col_off + cols, :]
            raw_out = raw_out + jnp.einsum(
                "trpi,io->trpo", window, w_taps[tap], preferred_element_type=jnp.float32
            )
            back = pad_grad[
                :, 2 - row_off : 2 - row_off + rows, 2 - col_off : 2 - col_off + cols, :
            ]
            grad_in = grad_in + jnp.einsum(
                "trpo,io->trpi", back, w_taps[tap], preferred_element_type=jnp.float32
            )
            mains.append(
                jnp.einsum("trpi,trpo->io", window, scaled, preferred_element_type=jnp.float32)
            )
    tile_grad = (grad_in * style[:, None, None, :]).astype(jnp.bfloat16)
    demod_dot = (
        live[:, None] * demod**3 * jnp.sum(out_grad.astype(jnp.float32) * raw_out, axis=(1, 2))
    )
    coupling = jnp.dot((style * style).T, demod_dot, precision=lax.Precision.HIGHEST)
    term = jnp.stack(mains) - w_taps.astype(jnp.float32) * coupling[None]
    return (tile_grad, term)


def per_device(tiles, out_grad, style, weight, tile_counts, crop_first):
    channels = weight.shape[1]
    slot_count = tiles.shape[0]
    devices = lax.axis_size("dp") * lax.axis_size("section")
    scale = 1.0 / (slot_count * devices * tiles.shape[1] * tiles.shape[2]) ** 0.5
    full_weight = lax.all_gather(weight, "dp", axis=0, tiled=True)
    w_taps = full_weight.reshape(9, channels, channels)
    w_float = w_taps.astype(jnp.float32)
    w_square = jnp.sum(w_float * w_float, axis=0)
    count = tile_counts[0]
    slot_ids = jnp.arange(slot_count, dtype=jnp.int32)
    live = (slot_ids < count).astype(jnp.float32)
    demod = lax.rsqrt(jnp.dot(style * style, w_square, precision=lax.Precision.HIGHEST) + 1e-08)
    modulated = (tiles.astype(jnp.float32) * style[:, None, None, :]).astype(jnp.bfloat16)
    scaled = (
        out_grad.astype(jnp.float32) * demod[:, None, None, :] * live[:, None, None, None]
    ).astype(jnp.bfloat16)
    edge = jnp.stack([modulated[:, -1], scaled[:, -1]], axis=1)
    head = jnp.stack([modulated[:, 0], scaled[:, 0]], axis=1)
    last_live = lax.dynamic_index_in_dim(edge, count - 1, 0, keepdims=False)
    recv_top = from_behind(last_live, ("dp", "section"), 1)
    first_sent = head[0] * (1 - crop_first[0]).astype(jnp.bfloat16)
    recv_bot = from_behind(first_sent, ("dp", "section"), -1)
    zero_slot = jnp.zeros((1,) + edge.shape[1:], jnp.bfloat16)
    top_local = jnp.concatenate([zero_slot, edge[:-1]], axis=0)
    top_mask = ((live > 0) & (crop_first == 0)).astype(jnp.bfloat16)
    top = (
        jnp.where((slot_ids == 0)[:, None, None, None], recv_top[None], top_local)
        * top_mask[:, None, None, None]
    )
    next_link = jnp.concatenate(
        [live[1:] * (1 - crop_first[1:]).astype(jnp.float32), jnp.zeros((1,), jnp.float32)], axis=0
    )
    bot_local = (
        jnp.concatenate([head[1:], zero_slot], axis=0)
        * next_link.astype(jnp.bfloat16)[:, None, None, None]
    )
    bottom = jnp.where((slot_ids == count - 1)[:, None, None, None], recv_bot[None], bot_local)
    tile_grad, term = tile_block(
        modulated, scaled, out_grad, style, live, demod, top, bottom, w_taps
    )
    flat_term = (term * scale).reshape(9 * channels, channels)
    shard = lax.psum_scatter(flat_term, "dp", scatter_dimension=0, tiled=True)
    weight_grad = lax.psum(shard, "section")
    return (tile_grad, weight_grad)


MESH = pl.DeviceIdType.MESH
F32 = jnp.float32
BF16 = jnp.bfloat16


def rolled(value, steps):
    wide = value.shape[0]
    place = lax.broadcasted_iota(jnp.int32, value.shape, 0)
    moved = pltpu.roll(value, steps % wide, 0)
    keep = (place >= steps) if steps > 0 else (place < wide + steps)
    return jnp.where(keep, moved, 0.0)


def fold(value):
    return value.reshape(value.shape[0] // 8, 8, value.shape[1]).sum(axis=0)


def fused_kernel(
    dps, secs, scale,
    count_hbm, first_hbm, tiles_hbm, g_hbm, style_hbm, w_hbm,
    tg_ref, wg_ref,
    count_ref, first_ref, tiles_ref, g_ref, style_ref, wfull, halo_out, halo_in, hdem_out, hdem_in, wsq, sq_all, norm_out, norm_in,
    pull_all, coup, modt, gcat, mains, wcat, scaled, facts, terms, crossing, pair_in, summed, rs_in,
    line_out, line_in, zin, fin,
    in_sem, h_ss, h_rs, sq_ss, sq_rs, sx_ss, sx_rs, nm_ss, nm_rs, pl_ss, pl_rs, px_ss, px_rs,
    wz_ss, wz_rs, wo_ss, wo_rs, wp_ss, wp_rs, sw_ss, sw_rs, p_ss, p_rs, r_ss, r_rs, l_ss, l_rs, zn_ss, zn_rs, a_ss, a_rs,
):
    slots, rows, cols, ch = tiles_ref.shape
    block = w_hbm.shape[0]
    half = block // 2
    lanes = ch // 2
    d = lax.axis_index("dp")
    s = lax.axis_index("section")
    n = d * secs + s
    total = dps * secs
    core = s % 2
    xc = s // 2
    zs = dps // 2
    z = d // 2
    y = d % 2

    def remote(src, dst, ss, rs, dp, sec):
        return pltpu.make_async_remote_copy(
            src_ref=src, dst_ref=dst, send_sem=ss, recv_sem=rs,
            device_id=(dp, sec), device_id_type=MESH,
        )

    def at(dz, dy, dx, dc):
        return ((z + dz) % zs) * 2 + (y + dy) % 2, ((xc + dx) % 2) * 2 + (core + dc) % 2

    after, before = (n + 1) % total, (n + total - 1) % total
    plane = ((1, 1), (1, 0), (0, 1))
    sibling = at(0, 0, 0, 1)
    other_y = at(0, 1, 0, 0)
    far = [3 - 3 * (z // 2), 2 - z // 2, z + 1 - 2 * (z % 2)]
    barrier = pltpu.get_barrier_semaphore()
    others = [far[j] * 2 + (y + dy) % 2 for j in range(zs - 1) for dy in (1, 0)] + [z * 2 + 1 - y]
    peers = [(owner, s) for owner in others] + [(d, (s + k) % secs) for k in range(1, secs)]
    peers += [at(0, 1, 1, 0), (after // secs, after % secs), (before // secs, before % secs)]
    for peer in peers:
        pl.semaphore_signal(barrier, inc=1, device_id=peer, device_id_type=MESH)

    mine = pl.ds(pl.multiple_of(block * d, 16), block)
    loads = [
        pltpu.make_async_copy(style_hbm, style_ref, in_sem.at[0]),
        pltpu.make_async_copy(w_hbm.at[:, 0:lanes], wfull.at[0, mine, :], in_sem.at[1]),
        pltpu.make_async_copy(w_hbm.at[:, lanes:ch], wfull.at[1, mine, :], in_sem.at[2]),
        pltpu.make_async_copy(tiles_hbm, tiles_ref, in_sem.at[3]),
        pltpu.make_async_copy(g_hbm, g_ref, in_sem.at[4]),
        pltpu.make_async_copy(count_hbm, count_ref, in_sem.at[5]),
        pltpu.make_async_copy(first_hbm, first_ref, in_sem.at[6]),
    ]
    for load in loads:
        load.start()
    sends = []

    def send(copy):
        copy.start()
        sends.append(copy)

    loads[0].wait()
    square = style_ref[...] * style_ref[...]
    sq_all[s, d, 0:slots, :] = square[:, :lanes]
    sq_all[s, d, slots : 2 * slots, :] = square[:, lanes:]
    pl.semaphore_wait(barrier, len(peers))

    def spread(ref, ss, rs):
        for i, owner in enumerate(others):
            send(remote(ref.at[s, d], ref.at[s, d], ss.at[i], rs.at[d], owner, s))

    def collect(ref, ss, rs):
        for i, owner in enumerate(others):
            remote(ref.at[s, owner], ref.at[s, owner], ss.at[i], rs.at[owner], owner, s).wait_recv()

    spread(sq_all, sq_ss, sq_rs)
    loads[3].wait()
    loads[4].wait()
    loads[5].wait()
    loads[6].wait()
    count = count_ref[0]
    row_t = tiles_ref[0, rows - 1].astype(F32)
    row_g = g_ref[0, rows - 1].astype(F32)
    row_s = style_ref[0:1, :]
    for t in range(1, slots):
        here = count - 1 == t
        row_t = jnp.where(here, tiles_ref[t, rows - 1].astype(F32), row_t)
        row_g = jnp.where(here, g_ref[t, rows - 1].astype(F32), row_g)
        row_s = jnp.where(here, style_ref[t : t + 1, :], row_s)
    halo_out[0, 0] = (row_t * row_s).astype(BF16)
    halo_out[0, 1] = row_g.astype(BF16)
    open_first = (1 - first_ref[0]).astype(F32)
    halo_out[1, 0] = (tiles_ref[0, 0].astype(F32) * style_ref[0:1, :] * open_first).astype(BF16)
    halo_out[1, 1] = (g_ref[0, 0].astype(F32) * open_first).astype(BF16)
    ways = ((after, n < total - 1, n > 0), (before, n > 0, n < total - 1))
    halos = []
    for way, (to, _, _) in enumerate(ways):
        halos.append([
            remote(halo_out.at[way], halo_in.at[way], h_ss.at[way], h_rs.at[way], to // secs, to % secs),
            remote(hdem_out.at[way], hdem_in.at[way], h_ss.at[2 + way], h_rs.at[2 + way], to // secs, to % secs),
        ])
    for way, (_, gives, takes) in enumerate(ways):
        @pl.when(gives)
        def _(way=way):
            halos[way][0].start()

        @pl.when(jnp.logical_not(takes))
        def _(way=way):
            halo_in[way] = jnp.zeros_like(halo_in[way])
            hdem_in[way] = jnp.zeros_like(hdem_in[way])

    loads[1].wait()
    loads[2].wait()

    def w_part(owner, which):
        return wfull.at[core, pl.ds(pl.multiple_of(block * owner + half * which, 16), half), :]

    for j in (2, 1, 0):
        send(remote(w_part(d, xc), w_part(d, xc), wz_ss.at[j], wz_rs.at[z], far[j] * 2 + y, s))
    own_w = wfull.at[core, mine, :]
    send(remote(own_w, own_w, wo_ss.at[0], wo_rs.at[0], *other_y))

    for h in range(2):
        w_own = wfull[h, mine, :].astype(F32)
        w_own = w_own * w_own
        folded = jnp.concatenate([w_own[: block - ch] + w_own[ch:], w_own[block - ch : ch]], axis=0)
        wsq[0:ch, h * lanes : (h + 1) * lanes] = folded
        wsq[ch : 2 * ch, h * lanes : (h + 1) * lanes] = folded
    shift = (block * d) % ch

    def put_g(row, value):
        gcat[row, :, 0:ch] = rolled(value, -1).astype(BF16)
        gcat[row, :, ch : 2 * ch] = value.astype(BF16)
        gcat[row, :, 2 * ch : 3 * ch] = rolled(value, 1).astype(BF16)

    def prepare(t, carry):
        row_style = style_ref[pl.ds(t, 1), :]
        for r in range(rows):
            value = (tiles_ref[t, r].astype(F32) * row_style).astype(BF16)
            modt[t, :, (r + 1) * cols : (r + 2) * cols] = value.T
            put_g(t * rows + r, g_ref[t, r].astype(F32))
        return carry

    lax.fori_loop(0, slots, prepare, 0)

    live = [(t < count).astype(F32) for t in range(slots)]
    shut = [(first_ref[t] == 0).astype(F32) for t in range(slots)]
    top_on = [live[t] * shut[t] for t in range(slots)]
    top_on[0] = top_on[0] * (n > 0).astype(F32)
    next_on = [live[t + 1] * shut[t + 1] for t in range(slots - 1)]
    last_on = [(count - 1 == t).astype(F32) * (n < total - 1).astype(F32) for t in range(slots)]

    def tile_mains(taps, t, carry):
        right = gcat[pl.ds(t * rows, rows)].reshape(rows * cols, 3 * ch)
        for a in taps:
            found = jnp.dot(modt[t, :, a * cols : (a + rows) * cols], right, preferred_element_type=F32)
            for b in range(3):
                tap = 3 * a + b
                mains[t, tap * ch : (tap + 1) * ch, :] = found[:, b * ch : (b + 1) * ch]
        return carry

    lax.fori_loop(0, slots, functools.partial(tile_mains, (1,)), 0)

    def w_forward(j):
        place = w_part(far[j] * 2 + y, xc)
        remote(place, place, wz_ss.at[j], wz_rs.at[far[j]], far[j] * 2 + y, s).wait_recv()
        for m, (dy, dx) in enumerate(plane):
            send(remote(place, place, wp_ss.at[3 * j + m], wp_rs.at[3 * far[j] + m], *at(0, dy, dx, 0)))

    w_forward(2)
    collect(sq_all, sq_ss, sq_rs)
    wide = dps * 2 * slots
    squares = sq_all[s].reshape(wide, lanes)
    aligned = wsq[pl.ds(pl.multiple_of(ch - shift, 16), ch), :]
    low = jnp.dot(squares, aligned[:lanes], precision=lax.Precision.HIGHEST, preferred_element_type=F32)
    high = jnp.dot(squares, aligned[lanes:], precision=lax.Precision.HIGHEST, preferred_element_type=F32)
    both = low + pltpu.roll(high, wide - slots, 0)
    upper = lax.broadcasted_iota(jnp.int32, (wide, lanes), 0) % (2 * slots) < slots
    packed = jnp.where(upper, both[:, :lanes], pltpu.roll(both[:, lanes:], slots, 0))
    norm_out[...] = packed.reshape(dps, 2 * slots, lanes)
    for i, owner in enumerate(others):
        send(remote(norm_out.at[owner], norm_in.at[d], nm_ss.at[i], nm_rs.at[d], owner, s))
    norm_in[d] = norm_out[d]
    for k in range(1, secs):
        send(remote(sq_all.at[s], sq_all.at[s], sx_ss.at[k - 1], sx_rs.at[k - 1], d, (s + k) % secs))

    w_forward(1)
    for way, (_, _, takes) in enumerate(ways):
        @pl.when(takes)
        def _(way=way):
            halos[way][0].wait_recv()

    put_g(slots * rows, halo_in[0, 1].astype(F32))
    put_g(slots * rows + 1, halo_in[1, 1].astype(F32))
    from_prev = halo_in[0, 0].T.astype(F32)
    from_next = halo_in[1, 0].T.astype(F32)
    for t in range(slots):
        above = from_prev if t == 0 else modt[t - 1, :, rows * cols : (rows + 1) * cols].astype(F32)
        modt[t, :, 0:cols] = (above * top_on[t]).astype(BF16)
        below = from_next * last_on[t]
        if t < slots - 1:
            below = below + modt[t + 1, :, cols : 2 * cols].astype(F32) * next_on[t]
        modt[t, :, (rows + 1) * cols : (rows + 2) * cols] = below.astype(BF16)

    lax.fori_loop(0, 1, functools.partial(tile_mains, (0, 2)), 0)
    w_forward(0)
    lax.fori_loop(1, slots, functools.partial(tile_mains, (0, 2)), 0)

    chunk = 2 * block

    def group(zd, which):
        return wfull.at[which, pl.ds(pl.multiple_of(chunk * zd, 16), chunk), :]

    def other_block(which):
        return wfull.at[which, pl.ds(pl.multiple_of(block * (2 * z + 1 - y), 16), block), :]

    def w_cross(j):
        for m, (dy, dx) in enumerate(plane):
            place = w_part(far[j] * 2 + (y + dy) % 2, (xc + dx) % 2)
            remote(place, place, wp_ss.at[3 * j + m], wp_rs.at[3 * far[j] + m], *at(0, dy, dx, 0)).wait_recv()
        send(remote(group(far[j], core), group(far[j], core), sw_ss.at[j], sw_rs.at[far[j]], *sibling))

    remote(other_block(core), other_block(core), wo_ss.at[0], wo_rs.at[0], *other_y).wait_recv()
    send(remote(other_block(core), other_block(core), sw_ss.at[zs - 1], sw_rs.at[z], *sibling))
    w_cross(2)
    for i, owner in enumerate(others):
        remote(norm_out.at[owner], norm_in.at[owner], nm_ss.at[i], nm_rs.at[owner], owner, s).wait_recv()
    inverse = lax.rsqrt(norm_in[...].sum(axis=0) + 1e-08)
    demod = [
        jnp.concatenate([inverse[t : t + 1, :], inverse[slots + t : slots + t + 1, :]], axis=1)
        for t in range(slots)
    ]
    gain = [demod[t] * live[t] * scale for t in range(slots)]
    for t in range(slots):
        facts[t : t + 1, :] = demod[t] * live[t]

    last = demod[0]
    for t in range(1, slots):
        last = jnp.where(count - 1 == t, demod[t], last)
    hdem_out[0] = jnp.broadcast_to(last, (8, ch))
    hdem_out[1] = jnp.broadcast_to(demod[0], (8, ch))
    for way, (_, gives, _) in enumerate(ways):
        @pl.when(gives)
        def _(way=way):
            halos[way][1].start()

    part = 64
    steps = chunk // part

    def term(k, carry):
        here = pl.ds(pl.multiple_of(k * part, part), part)
        value = sum(gain[t] * mains[t, here, :] for t in range(slots))
        terms[here, :] = jnp.where(core == 0, value[:, :lanes], value[:, lanes:])
        crossing[here, :] = jnp.where(core == 0, value[:, lanes:], value[:, :lanes]).astype(BF16)
        return carry

    order = [far[0], far[2], far[1], z]
    pairs = []
    for i, zd in enumerate(order):
        lax.fori_loop(zd * steps, (zd + 1) * steps, term, 0)
        span = pl.ds(pl.multiple_of(chunk * zd, 64), chunk)
        pairs.append(remote(crossing.at[span, :], pair_in.at[span, :], p_ss.at[i], p_rs.at[i], *sibling))
        pairs[i].start()

    def share(zd, dy, dx, low=0):
        row = chunk * zd + block * ((y + dy) % 2) + half * ((xc + dx) % 2) + low
        return pl.ds(pl.multiple_of(row, 16), half - low)

    shares = []

    def plane_send(i, zd, low=0):
        size = half - low
        for m, (dy, dx) in enumerate(plane):
            copy = remote(
                summed.at[share(zd, dy, dx, low), :], rs_in.at[i, m, 0:size, :], r_ss.at[3 * i + m], r_rs.at[3 * i + m],
                *at(0, dy, dx, 0)
            )
            copy.start()
            shares.append(copy)

    early = half * 2 // 3 // 16 * 16
    hops = []
    for q in range(4):
        source = summed.at[pl.ds(pl.multiple_of(chunk * far[2] + half * q, 16), early), :]
        place = zin.at[half * q : half * q + early, :]
        hops.append(remote(source, place, zn_ss.at[q], zn_rs.at[q], far[2] * 2 + y, s))
    for i, zd in enumerate(order):
        pairs[i].wait_recv()

        def add_pair(m, carry, zd=zd):
            here = pl.ds(pl.multiple_of(zd * chunk + m * part, part), part)
            summing = terms[here, :] + pair_in[here, :].astype(F32)
            terms[here, :] = summing
            summed[here, :] = summing.astype(BF16)
            return carry

        lax.fori_loop(0, steps, add_pair, 0)
        if i == 1:
            for hop in hops:
                send(hop)
        elif i < zs - 1:
            plane_send(i // 2, zd)
    plane_send(zs - 2, far[2], early)

    def rescale(t, carry):
        factor = facts[pl.ds(t, 1), :]
        for r in range(rows):
            for b in range(3):
                tap = slice(b * ch, (b + 1) * ch)
                scaled[t, r + 1, :, tap] = (gcat[t * rows + r, :, tap].astype(F32) * factor).astype(BF16)
        return carry

    w_cross(1)
    w_cross(0)
    lax.fori_loop(0, slots, rescale, 0)
    remote(other_block(1 - core), other_block(1 - core), sw_ss.at[zs - 1], sw_rs.at[z], *sibling).wait_recv()
    for j in (2, 1, 0):
        place = group(far[j], 1 - core)
        remote(place, place, sw_ss.at[j], sw_rs.at[far[j]], *sibling).wait_recv()

    def sums(k, dots):
        here = pl.ds(pl.multiple_of(k * part, part), part)
        wv = jnp.concatenate([wfull[0, here, :], wfull[1, here, :]], axis=1).astype(F32)
        return tuple(dots[t] + fold(wv * mains[t, here, :]) for t in range(slots))

    zero = jnp.zeros((8, ch), F32)
    dots = lax.fori_loop(0, 9 * ch // part, sums, (zero,) * slots)
    for t in range(slots):
        pull = live[t] * demod[t] * demod[t] * demod[t] * jnp.sum(dots[t], axis=0, keepdims=True) * scale
        pull_all[s, d, t : t + 1, :] = pull[:, :lanes]
        pull_all[s, d, slots + t : slots + t + 1, :] = pull[:, lanes:]
    spread(pull_all, pl_ss, pl_rs)

    for way, (_, _, takes) in enumerate(ways):
        @pl.when(takes)
        def _(way=way):
            halos[way][1].wait_recv()

    def edges():
        for t in range(slots):
            for b in range(3):
                tap = slice(b * ch, (b + 1) * ch)
                above, factor = (slots * rows, hdem_in[0, 0:1, :]) if t == 0 else (t * rows - 1, demod[t - 1])
                scaled[t, 0, :, tap] = (gcat[above, :, tap].astype(F32) * (factor * top_on[t])).astype(BF16)
                below = gcat[slots * rows + 1, :, tap].astype(F32) * (hdem_in[1, 0:1, :] * last_on[t])
                if t < slots - 1:
                    below = below + gcat[(t + 1) * rows, :, tap].astype(F32) * (demod[t + 1] * next_on[t])
                scaled[t, rows + 1, :, tap] = below.astype(BF16)
        for a in range(3):
            for b in range(3):
                tap = 3 * a + b
                for h in range(2):
                    wcat[a, :, b * ch + h * lanes : b * ch + (h + 1) * lanes] = wfull[h, tap * ch : (tap + 1) * ch, :]

    def tile_back(t, carry):
        found = None
        for a in range(3):
            left = scaled[t, 2 - a : 2 - a + rows].reshape(rows * cols, 3 * ch)
            more = lax.dot_general(left, wcat[a], (((1,), (1,)), ((), ())), preferred_element_type=F32)
            found = more if found is None else found + more
        found = (found * style_ref[pl.ds(t, 1), :]).astype(BF16)
        tg_ref[t] = found.reshape(rows, cols, ch)
        return carry

    for q, hop in enumerate(hops):
        hop.wait_recv()
        here = pl.ds(pl.multiple_of(chunk * z + half * q, 16), early)
        summing = terms[here, :] + zin[half * q : half * q + early, :].astype(F32)
        terms[here, :] = summing
        summed[here, :] = summing.astype(BF16)
    plane_send(zs - 1, z)
    edges()
    lines = []
    for i, zd in enumerate([far[0], far[1], far[2], z]):
        low = early if i == zs - 2 else 0
        size = half - low
        own = terms[share(zd, 0, 0, low), :]
        for m in range(3):
            shares[3 * i + m].wait_recv()
            own = own + rs_in[i, m, 0:size, :].astype(F32)
        if i < zs - 1:
            line_out[i, 0:size, :] = own.astype(BF16)
            place = line_in.at[z, 0:size, :]
            lines.append(remote(line_out.at[i, 0:size, :], place, l_ss.at[i], l_rs.at[z], zd * 2 + y, s))
            lines[-1].start()
        if i == zs - 2:
            lax.fori_loop(0, slots - 2, tile_back, 0)
            collect(pull_all, pl_ss, pl_rs)
            for k in range(1, secs):
                send(remote(pull_all.at[s], pull_all.at[s], px_ss.at[k - 1], px_rs.at[k - 1], d, (s + k) % secs))
            lax.fori_loop(slots - 2, slots, tile_back, 0)
    for j in (2, 1, 0):
        size = half - early if j == 2 else half
        place = line_in.at[far[j], 0:size, :]
        remote(line_out.at[j, 0:size, :], place, l_ss.at[j], l_rs.at[far[j]], far[j] * 2 + y, s).wait_recv()
        more = line_in[far[j], 0:size, :].astype(F32)
        own = jnp.concatenate([own[:early], own[early:] + more], axis=0) if j == 2 else own + more
    fin[s] = own.astype(BF16)
    gathers = []
    for k in range(1, secs):
        copy = remote(fin.at[s], fin.at[s], a_ss.at[k - 1], a_rs.at[k - 1], d, (s + k) % secs)
        copy.start()
        gathers.append(copy)

    for k in range(1, secs):
        for ref, ss, rs in ((sq_all, sx_ss, sx_rs), (pull_all, px_ss, px_rs)):
            place = ref.at[(s + secs - k) % secs]
            remote(place, place, ss.at[k - 1], rs.at[k - 1], d, (s + k) % secs).wait_recv()
    tall = secs * wide
    upper = lax.broadcasted_iota(jnp.int32, (tall, lanes), 0) % (2 * slots) < slots

    def unpacked(ref):
        value = ref[...].reshape(tall, lanes)
        moved = pltpu.roll(value, tall - slots, 0)
        return jnp.concatenate([jnp.where(upper, value, 0.0), jnp.where(upper, moved, 0.0)], axis=1)

    coupled = jnp.dot(
        unpacked(sq_all).T, unpacked(pull_all), precision=lax.Precision.HIGHEST, preferred_element_type=F32
    )
    coup[0:ch, :] = coupled
    coup[ch : 2 * ch, :] = coupled
    for q in range(secs):
        row, h = half * (q // 2), q % 2
        w_own = wfull[h, pl.ds(pl.multiple_of(block * d + row, 16), half), :].astype(F32)
        c_own = coup[pl.ds(pl.multiple_of(shift + row, 16), half), h * lanes : (h + 1) * lanes]
        wg_ref[row : row + half, h * lanes : (h + 1) * lanes] = w_own * c_own
    for k in range(1, secs):
        other = fin.at[(s + secs - k) % secs]
        remote(other, other, a_ss.at[k - 1], a_rs.at[k - 1], d, (s + k) % secs).wait_recv()
    for q in range(secs):
        row, h = half * (q // 2), q % 2
        span = (slice(row, row + half), slice(h * lanes, (h + 1) * lanes))
        wg_ref[span] = fin[q].astype(F32) - wg_ref[span]
    for way, (_, gives, _) in enumerate(ways):
        @pl.when(gives)
        def _(way=way):
            for copy in halos[way]:
                copy.wait_send()

    for copy in sends + pairs + shares + lines + gathers:
        copy.wait_send()


def store_kernel(tg_ref, wg_ref, tg_out, wg_out, t_sem, w_sem):
    copies = [pltpu.make_async_copy(tg_ref.at[t], tg_out.at[t], t_sem.at[t]) for t in range(tg_ref.shape[0])]
    copies.append(pltpu.make_async_copy(wg_ref, wg_out, w_sem))
    for copy in copies:
        copy.start()
    for copy in copies:
        copy.wait()


def fused(dps, secs, tiles, out_grad, style, weight, tile_counts, crop_first):
    slots, rows, cols, ch = tiles.shape
    block = weight.shape[0]
    half = block // 2
    lanes = ch // 2
    zs = dps // 2
    scale = 1.0 / (slots * dps * secs * rows * cols) ** 0.5
    dma = pltpu.SemaphoreType.DMA
    vmem = pl.BlockSpec(memory_space=pltpu.VMEM)
    hbm = pl.BlockSpec(memory_space=pltpu.HBM)
    counts = [dps - 1, dps, secs - 1, secs - 1, dps - 1, dps, dps - 1, dps, secs - 1, secs - 1]
    counts += [zs - 1, zs, 1, 1, 3 * zs - 3, 3 * zs, zs, zs, zs, zs, 3 * zs, 3 * zs, zs - 1, zs, 4, 4, secs - 1, secs - 1]
    tg, wg = pl.pallas_call(
        functools.partial(fused_kernel, dps, secs, scale),
        out_shape=(
            pltpu.VMEM(tiles.shape, BF16),
            pltpu.VMEM(weight.shape, F32),
        ),
        in_specs=[hbm] * 6,
        out_specs=(vmem, vmem),
        scratch_shapes=[
            pltpu.SMEM(tile_counts.shape, jnp.int32),
            pltpu.SMEM(crop_first.shape, jnp.int32),
            pltpu.VMEM(tiles.shape, BF16),
            pltpu.VMEM(tiles.shape, BF16),
            pltpu.VMEM(style.shape, F32),
            pltpu.VMEM((2, 9 * ch, lanes), BF16),
            pltpu.VMEM((2, 2, cols, ch), BF16),
            pltpu.VMEM((2, 2, cols, ch), BF16),
            pltpu.VMEM((2, 8, ch), F32),
            pltpu.VMEM((2, 8, ch), F32),
            pltpu.VMEM((2 * ch, ch), F32),
            pltpu.VMEM((secs, dps, 2 * slots, lanes), F32),
            pltpu.VMEM((dps, 2 * slots, lanes), F32),
            pltpu.VMEM((dps, 2 * slots, lanes), F32),
            pltpu.VMEM((secs, dps, 2 * slots, lanes), F32),
            pltpu.VMEM((2 * ch, ch), F32),
            pltpu.VMEM((slots, ch, (rows + 2) * cols), BF16),
            pltpu.VMEM((slots * rows + 2, cols, 3 * ch), BF16),
            pltpu.VMEM((slots, 9 * ch, ch), F32),
            pltpu.VMEM((3, ch, 3 * ch), BF16),
            pltpu.VMEM((slots, rows + 2, cols, 3 * ch), BF16),
            pltpu.VMEM((8, ch), F32),
            pltpu.VMEM((9 * ch, lanes), F32),
            pltpu.VMEM((9 * ch, lanes), BF16),
            pltpu.VMEM((9 * ch, lanes), BF16),
            pltpu.VMEM((9 * ch, lanes), BF16),
            pltpu.VMEM((zs, 3, half, lanes), BF16),
            pltpu.VMEM((zs - 1, half, lanes), BF16),
            pltpu.VMEM((zs, half, lanes), BF16),
            pltpu.VMEM((2 * block, lanes), BF16),
            pltpu.VMEM((secs, half, lanes), BF16),
            dma((7,)), dma((4,)), dma((4,)),
        ] + [dma((count,)) for count in counts],
        compiler_params=pltpu.CompilerParams(collective_id=0, has_side_effects=True, vmem_limit_bytes=56 * 1024 * 1024),
        name="fused_backward",
    )(tile_counts, crop_first, tiles, out_grad, style, weight)
    return pl.pallas_call(
        store_kernel,
        out_shape=(
            jax.ShapeDtypeStruct(tiles.shape, BF16),
            jax.ShapeDtypeStruct(weight.shape, F32),
        ),
        in_specs=[vmem, vmem],
        out_specs=(hbm, hbm),
        scratch_shapes=[dma((slots,)), dma],
        compiler_params=pltpu.CompilerParams(has_side_effects=True, vmem_limit_bytes=1024 * 1024),
        name="store_out",
    )(tg, wg)


def solution(mesh):
    placed = (
        P(("dp", "section"), None, None, None),
        P(("dp", "section"), None, None, None),
        P(("dp", "section"), None),
        P("dp", None),
        P(("dp", "section")),
        P(("dp", "section")),
    )
    dps, secs = mesh.shape["dp"], mesh.shape["section"]

    def body(tiles, out_grad, style, weight, tile_counts, crop_first):
        args = (tiles, out_grad, style, weight, tile_counts, crop_first)
        rows, ch = weight.shape
        if secs == 4 and dps == 8 and tiles.shape[0] == 4 and rows % 32 == 0 and ch <= rows < 2 * ch:
            return fused(dps, secs, *args)
        return per_device(*args)

    return jax.shard_map(
        body,
        mesh=mesh,
        in_specs=placed,
        out_specs=(P(("dp", "section"), None, None, None), P("dp", None)),
        check_vma=False,
    )
```

```python
import functools

import jax
import jax.numpy as jnp
from jax import lax
from jax.experimental import pallas as pl
from jax.experimental.pallas import tpu as pltpu
from jax.sharding import PartitionSpec as P


def from_behind(value, axis, steps):
    count = lax.axis_size(axis)
    leading, last = (max(0, -steps), min(count, count - steps))
    return lax.ppermute(value, axis, [(source, source + steps) for source in range(leading, last)])


def tile_block(modulated, scaled, out_grad, style, live, demod, top, bottom, w_taps):
    rows = modulated.shape[1]
    cols = modulated.shape[2]
    ext_mod = jnp.concatenate([top[:, 0][:, None], modulated, bottom[:, 0][:, None]], axis=1)
    ext_grad = jnp.concatenate([top[:, 1][:, None], scaled, bottom[:, 1][:, None]], axis=1)
    pad_mod = jnp.pad(ext_mod, ((0, 0), (0, 0), (1, 1), (0, 0)))
    pad_grad = jnp.pad(ext_grad, ((0, 0), (0, 0), (1, 1), (0, 0)))
    raw_out = jnp.zeros(out_grad.shape, jnp.float32)
    grad_in = jnp.zeros(modulated.shape, jnp.float32)
    mains = []
    for row_off in range(3):
        for col_off in range(3):
            tap = row_off * 3 + col_off
            window = pad_mod[:, row_off : row_off + rows, col_off : col_off + cols, :]
            raw_out = raw_out + jnp.einsum(
                "trpi,io->trpo", window, w_taps[tap], preferred_element_type=jnp.float32
            )
            back = pad_grad[
                :, 2 - row_off : 2 - row_off + rows, 2 - col_off : 2 - col_off + cols, :
            ]
            grad_in = grad_in + jnp.einsum(
                "trpo,io->trpi", back, w_taps[tap], preferred_element_type=jnp.float32
            )
            mains.append(
                jnp.einsum("trpi,trpo->io", window, scaled, preferred_element_type=jnp.float32)
            )
    tile_grad = (grad_in * style[:, None, None, :]).astype(jnp.bfloat16)
    demod_dot = (
        live[:, None] * demod**3 * jnp.sum(out_grad.astype(jnp.float32) * raw_out, axis=(1, 2))
    )
    coupling = jnp.dot((style * style).T, demod_dot, precision=lax.Precision.HIGHEST)
    term = jnp.stack(mains) - w_taps.astype(jnp.float32) * coupling[None]
    return (tile_grad, term)


def per_device(tiles, out_grad, style, weight, tile_counts, crop_first):
    channels = weight.shape[1]
    slot_count = tiles.shape[0]
    devices = lax.axis_size("dp") * lax.axis_size("section")
    scale = 1.0 / (slot_count * devices * tiles.shape[1] * tiles.shape[2]) ** 0.5
    full_weight = lax.all_gather(weight, "dp", axis=0, tiled=True)
    w_taps = full_weight.reshape(9, channels, channels)
    w_float = w_taps.astype(jnp.float32)
    w_square = jnp.sum(w_float * w_float, axis=0)
    count = tile_counts[0]
    slot_ids = jnp.arange(slot_count, dtype=jnp.int32)
    live = (slot_ids < count).astype(jnp.float32)
    demod = lax.rsqrt(jnp.dot(style * style, w_square, precision=lax.Precision.HIGHEST) + 1e-08)
    modulated = (tiles.astype(jnp.float32) * style[:, None, None, :]).astype(jnp.bfloat16)
    scaled = (
        out_grad.astype(jnp.float32) * demod[:, None, None, :] * live[:, None, None, None]
    ).astype(jnp.bfloat16)
    edge = jnp.stack([modulated[:, -1], scaled[:, -1]], axis=1)
    head = jnp.stack([modulated[:, 0], scaled[:, 0]], axis=1)
    last_live = lax.dynamic_index_in_dim(edge, count - 1, 0, keepdims=False)
    recv_top = from_behind(last_live, ("dp", "section"), 1)
    first_sent = head[0] * (1 - crop_first[0]).astype(jnp.bfloat16)
    recv_bot = from_behind(first_sent, ("dp", "section"), -1)
    zero_slot = jnp.zeros((1,) + edge.shape[1:], jnp.bfloat16)
    top_local = jnp.concatenate([zero_slot, edge[:-1]], axis=0)
    top_mask = ((live > 0) & (crop_first == 0)).astype(jnp.bfloat16)
    top = (
        jnp.where((slot_ids == 0)[:, None, None, None], recv_top[None], top_local)
        * top_mask[:, None, None, None]
    )
    next_link = jnp.concatenate(
        [live[1:] * (1 - crop_first[1:]).astype(jnp.float32), jnp.zeros((1,), jnp.float32)], axis=0
    )
    bot_local = (
        jnp.concatenate([head[1:], zero_slot], axis=0)
        * next_link.astype(jnp.bfloat16)[:, None, None, None]
    )
    bottom = jnp.where((slot_ids == count - 1)[:, None, None, None], recv_bot[None], bot_local)
    tile_grad, term = tile_block(
        modulated, scaled, out_grad, style, live, demod, top, bottom, w_taps
    )
    flat_term = (term * scale).reshape(9 * channels, channels)
    shard = lax.psum_scatter(flat_term, "dp", scatter_dimension=0, tiled=True)
    weight_grad = lax.psum(shard, "section")
    return (tile_grad, weight_grad)


MESH = pl.DeviceIdType.MESH
F32 = jnp.float32
BF16 = jnp.bfloat16


def rolled(value, steps):
    wide = value.shape[0]
    place = lax.broadcasted_iota(jnp.int32, value.shape, 0)
    moved = pltpu.roll(value, steps % wide, 0)
    keep = (place >= steps) if steps > 0 else (place < wide + steps)
    return jnp.where(keep, moved, 0.0)


def fold(value):
    return value.reshape(value.shape[0] // 8, 8, value.shape[1]).sum(axis=0)


def fused_kernel(
    dps, secs, scale,
    count_hbm, first_hbm, tiles_hbm, g_hbm, style_hbm, w_hbm,
    tg_ref, wg_ref,
    count_ref, first_ref, tiles_ref, g_ref, style_ref, wfull, halo_out, halo_in, hdem_out, hdem_in, wsq, sq_all, norm_out, norm_in,
    pull_all, coup, modt, gcat, mains, wcat, scaled, facts, terms, crossing, pair_in, summed, rs_in,
    line_out, line_in, zin, fin,
    in_sem, h_ss, h_rs, sq_ss, sq_rs, sx_ss, sx_rs, nm_ss, nm_rs, pl_ss, pl_rs, px_ss, px_rs,
    wz_ss, wz_rs, wo_ss, wo_rs, wp_ss, wp_rs, sw_ss, sw_rs, p_ss, p_rs, r_ss, r_rs, l_ss, l_rs, zn_ss, zn_rs, a_ss, a_rs,
):
    slots, rows, cols, ch = tiles_ref.shape
    block = w_hbm.shape[0]
    half = block // 2
    lanes = ch // 2
    d = lax.axis_index("dp")
    s = lax.axis_index("section")
    n = d * secs + s
    total = dps * secs
    core = s % 2
    xc = s // 2
    zs = dps // 2
    z = d // 2
    y = d % 2

    def remote(src, dst, ss, rs, dp, sec):
        return pltpu.make_async_remote_copy(
            src_ref=src, dst_ref=dst, send_sem=ss, recv_sem=rs,
            device_id=(dp, sec), device_id_type=MESH,
        )

    def at(dz, dy, dx, dc):
        return ((z + dz) % zs) * 2 + (y + dy) % 2, ((xc + dx) % 2) * 2 + (core + dc) % 2

    after, before = (n + 1) % total, (n + total - 1) % total
    plane = ((1, 1), (1, 0), (0, 1))
    sibling = at(0, 0, 0, 1)
    other_y = at(0, 1, 0, 0)
    far = [3 - 3 * (z // 2), 2 - z // 2, z + 1 - 2 * (z % 2)]
    barrier = pltpu.get_barrier_semaphore()
    others = [far[j] * 2 + (y + dy) % 2 for j in range(zs - 1) for dy in (1, 0)] + [z * 2 + 1 - y]
    peers = [(owner, s) for owner in others] + [(d, (s + k) % secs) for k in range(1, secs)]
    peers += [at(0, 1, 1, 0), (after // secs, after % secs), (before // secs, before % secs)]

    mine = pl.ds(pl.multiple_of(block * d, 16), block)
    loads = [
        pltpu.make_async_copy(style_hbm, style_ref, in_sem.at[0]),
        pltpu.make_async_copy(w_hbm.at[:, 0:lanes], wfull.at[0, mine, :], in_sem.at[1]),
        pltpu.make_async_copy(w_hbm.at[:, lanes:ch], wfull.at[1, mine, :], in_sem.at[2]),
        pltpu.make_async_copy(tiles_hbm, tiles_ref, in_sem.at[3]),
        pltpu.make_async_copy(g_hbm, g_ref, in_sem.at[4]),
        pltpu.make_async_copy(count_hbm, count_ref, in_sem.at[5]),
        pltpu.make_async_copy(first_hbm, first_ref, in_sem.at[6]),
    ]
    loads[0].start()
    for peer in peers:
        pl.semaphore_signal(barrier, inc=1, device_id=peer, device_id_type=MESH)
    for load in loads[1:]:
        load.start()
    sends = []

    def send(copy):
        copy.start()
        sends.append(copy)

    loads[0].wait()
    square = style_ref[...] * style_ref[...]
    sq_all[s, d, 0:slots, :] = square[:, :lanes]
    sq_all[s, d, slots : 2 * slots, :] = square[:, lanes:]
    loads[3].wait()
    loads[4].wait()
    loads[5].wait()
    loads[6].wait()
    count = count_ref[0]
    row_t = tiles_ref[0, rows - 1].astype(F32)
    row_g = g_ref[0, rows - 1].astype(F32)
    row_s = style_ref[0:1, :]
    for t in range(1, slots):
        here = count - 1 == t
        row_t = jnp.where(here, tiles_ref[t, rows - 1].astype(F32), row_t)
        row_g = jnp.where(here, g_ref[t, rows - 1].astype(F32), row_g)
        row_s = jnp.where(here, style_ref[t : t + 1, :], row_s)
    halo_out[0, 0] = (row_t * row_s).astype(BF16)
    halo_out[0, 1] = row_g.astype(BF16)
    open_first = (1 - first_ref[0]).astype(F32)
    halo_out[1, 0] = (tiles_ref[0, 0].astype(F32) * style_ref[0:1, :] * open_first).astype(BF16)
    halo_out[1, 1] = (g_ref[0, 0].astype(F32) * open_first).astype(BF16)
    loads[1].wait()
    loads[2].wait()
    for h in range(2):
        w_own = wfull[h, mine, :].astype(F32)
        w_own = w_own * w_own
        folded = jnp.concatenate([w_own[: block - ch] + w_own[ch:], w_own[block - ch : ch]], axis=0)
        wsq[0:ch, h * lanes : (h + 1) * lanes] = folded
        wsq[ch : 2 * ch, h * lanes : (h + 1) * lanes] = folded
    pl.semaphore_wait(barrier, len(peers))

    def spread(ref, ss, rs):
        for i, owner in enumerate(others):
            send(remote(ref.at[s, d], ref.at[s, d], ss.at[i], rs.at[d], owner, s))

    def collect(ref, ss, rs):
        for i, owner in enumerate(others):
            remote(ref.at[s, owner], ref.at[s, owner], ss.at[i], rs.at[owner], owner, s).wait_recv()

    spread(sq_all, sq_ss, sq_rs)
    ways = ((after, n < total - 1, n > 0), (before, n > 0, n < total - 1))
    halos = []
    for way, (to, _, _) in enumerate(ways):
        halos.append([
            remote(halo_out.at[way], halo_in.at[way], h_ss.at[way], h_rs.at[way], to // secs, to % secs),
            remote(hdem_out.at[way], hdem_in.at[way], h_ss.at[2 + way], h_rs.at[2 + way], to // secs, to % secs),
        ])
    for way, (_, gives, takes) in enumerate(ways):
        @pl.when(gives)
        def _(way=way):
            halos[way][0].start()

        @pl.when(jnp.logical_not(takes))
        def _(way=way):
            halo_in[way] = jnp.zeros_like(halo_in[way])
            hdem_in[way] = jnp.zeros_like(hdem_in[way])


    def w_part(owner, which):
        return wfull.at[core, pl.ds(pl.multiple_of(block * owner + half * which, 16), half), :]

    for j in (2, 1, 0):
        send(remote(w_part(d, xc), w_part(d, xc), wz_ss.at[j], wz_rs.at[z], far[j] * 2 + y, s))
    own_w = wfull.at[core, mine, :]
    send(remote(own_w, own_w, wo_ss.at[0], wo_rs.at[0], *other_y))

    shift = (block * d) % ch

    def put_g(row, value):
        gcat[row, :, 0:ch] = rolled(value, -1).astype(BF16)
        gcat[row, :, ch : 2 * ch] = value.astype(BF16)
        gcat[row, :, 2 * ch : 3 * ch] = rolled(value, 1).astype(BF16)

    def prepare(t, carry):
        row_style = style_ref[pl.ds(t, 1), :]
        for r in range(rows):
            value = (tiles_ref[t, r].astype(F32) * row_style).astype(BF16)
            modt[t, :, (r + 1) * cols : (r + 2) * cols] = value.T
            put_g(t * rows + r, g_ref[t, r].astype(F32))
        return carry

    lax.fori_loop(0, slots, prepare, 0)

    live = [(t < count).astype(F32) for t in range(slots)]
    shut = [(first_ref[t] == 0).astype(F32) for t in range(slots)]
    top_on = [live[t] * shut[t] for t in range(slots)]
    top_on[0] = top_on[0] * (n > 0).astype(F32)
    next_on = [live[t + 1] * shut[t + 1] for t in range(slots - 1)]
    last_on = [(count - 1 == t).astype(F32) * (n < total - 1).astype(F32) for t in range(slots)]

    def tile_mains(taps, t, carry):
        right = gcat[pl.ds(t * rows, rows)].reshape(rows * cols, 3 * ch)
        for a in taps:
            found = jnp.dot(modt[t, :, a * cols : (a + rows) * cols], right, preferred_element_type=F32)
            for b in range(3):
                tap = 3 * a + b
                mains[t, tap * ch : (tap + 1) * ch, :] = found[:, b * ch : (b + 1) * ch]
        return carry

    lax.fori_loop(0, slots, functools.partial(tile_mains, (1,)), 0)

    def w_forward(j):
        place = w_part(far[j] * 2 + y, xc)
        remote(place, place, wz_ss.at[j], wz_rs.at[far[j]], far[j] * 2 + y, s).wait_recv()
        for m, (dy, dx) in enumerate(plane):
            send(remote(place, place, wp_ss.at[3 * j + m], wp_rs.at[3 * far[j] + m], *at(0, dy, dx, 0)))

    w_forward(2)
    collect(sq_all, sq_ss, sq_rs)
    wide = dps * 2 * slots
    squares = sq_all[s].reshape(wide, lanes)
    aligned = wsq[pl.ds(pl.multiple_of(ch - shift, 16), ch), :]
    low = jnp.dot(squares, aligned[:lanes], precision=lax.Precision.HIGHEST, preferred_element_type=F32)
    high = jnp.dot(squares, aligned[lanes:], precision=lax.Precision.HIGHEST, preferred_element_type=F32)
    both = low + pltpu.roll(high, wide - slots, 0)
    upper = lax.broadcasted_iota(jnp.int32, (wide, lanes), 0) % (2 * slots) < slots
    packed = jnp.where(upper, both[:, :lanes], pltpu.roll(both[:, lanes:], slots, 0))
    norm_out[...] = packed.reshape(dps, 2 * slots, lanes)
    for i, owner in enumerate(others):
        send(remote(norm_out.at[owner], norm_in.at[d], nm_ss.at[i], nm_rs.at[d], owner, s))
    norm_in[d] = norm_out[d]
    for k in range(1, secs):
        send(remote(sq_all.at[s], sq_all.at[s], sx_ss.at[k - 1], sx_rs.at[k - 1], d, (s + k) % secs))

    w_forward(1)
    for way, (_, _, takes) in enumerate(ways):
        @pl.when(takes)
        def _(way=way):
            halos[way][0].wait_recv()

    put_g(slots * rows, halo_in[0, 1].astype(F32))
    put_g(slots * rows + 1, halo_in[1, 1].astype(F32))
    from_prev = halo_in[0, 0].T.astype(F32)
    from_next = halo_in[1, 0].T.astype(F32)
    for t in range(slots):
        above = from_prev if t == 0 else modt[t - 1, :, rows * cols : (rows + 1) * cols].astype(F32)
        modt[t, :, 0:cols] = (above * top_on[t]).astype(BF16)
        below = from_next * last_on[t]
        if t < slots - 1:
            below = below + modt[t + 1, :, cols : 2 * cols].astype(F32) * next_on[t]
        modt[t, :, (rows + 1) * cols : (rows + 2) * cols] = below.astype(BF16)

    lax.fori_loop(0, 1, functools.partial(tile_mains, (0, 2)), 0)
    w_forward(0)
    lax.fori_loop(1, slots, functools.partial(tile_mains, (0, 2)), 0)

    chunk = 2 * block

    def group(zd, which):
        return wfull.at[which, pl.ds(pl.multiple_of(chunk * zd, 16), chunk), :]

    def other_block(which):
        return wfull.at[which, pl.ds(pl.multiple_of(block * (2 * z + 1 - y), 16), block), :]

    def w_cross(j):
        for m, (dy, dx) in enumerate(plane):
            place = w_part(far[j] * 2 + (y + dy) % 2, (xc + dx) % 2)
            remote(place, place, wp_ss.at[3 * j + m], wp_rs.at[3 * far[j] + m], *at(0, dy, dx, 0)).wait_recv()
        send(remote(group(far[j], core), group(far[j], core), sw_ss.at[j], sw_rs.at[far[j]], *sibling))

    remote(other_block(core), other_block(core), wo_ss.at[0], wo_rs.at[0], *other_y).wait_recv()
    send(remote(other_block(core), other_block(core), sw_ss.at[zs - 1], sw_rs.at[z], *sibling))
    w_cross(2)
    for i, owner in enumerate(others):
        remote(norm_out.at[owner], norm_in.at[owner], nm_ss.at[i], nm_rs.at[owner], owner, s).wait_recv()
    inverse = lax.rsqrt(norm_in[...].sum(axis=0) + 1e-08)
    demod = [
        jnp.concatenate([inverse[t : t + 1, :], inverse[slots + t : slots + t + 1, :]], axis=1)
        for t in range(slots)
    ]
    gain = [demod[t] * live[t] * scale for t in range(slots)]
    for t in range(slots):
        facts[t : t + 1, :] = demod[t] * live[t]

    last = demod[0]
    for t in range(1, slots):
        last = jnp.where(count - 1 == t, demod[t], last)
    hdem_out[0] = jnp.broadcast_to(last, (8, ch))
    hdem_out[1] = jnp.broadcast_to(demod[0], (8, ch))
    for way, (_, gives, _) in enumerate(ways):
        @pl.when(gives)
        def _(way=way):
            halos[way][1].start()

    part = 64
    steps = chunk // part

    def term(k, carry):
        here = pl.ds(pl.multiple_of(k * part, part), part)
        value = sum(gain[t] * mains[t, here, :] for t in range(slots))
        terms[here, :] = jnp.where(core == 0, value[:, :lanes], value[:, lanes:])
        crossing[here, :] = jnp.where(core == 0, value[:, lanes:], value[:, :lanes]).astype(BF16)
        return carry

    order = [far[0], far[2], far[1], z]
    pairs = []
    for i, zd in enumerate(order):
        lax.fori_loop(zd * steps, (zd + 1) * steps, term, 0)
        span = pl.ds(pl.multiple_of(chunk * zd, 64), chunk)
        pairs.append(remote(crossing.at[span, :], pair_in.at[span, :], p_ss.at[i], p_rs.at[i], *sibling))
        pairs[i].start()

    def share(zd, dy, dx, low=0):
        row = chunk * zd + block * ((y + dy) % 2) + half * ((xc + dx) % 2) + low
        return pl.ds(pl.multiple_of(row, 16), half - low)

    shares = []

    def plane_send(i, zd, low=0):
        size = half - low
        for m, (dy, dx) in enumerate(plane):
            copy = remote(
                summed.at[share(zd, dy, dx, low), :], rs_in.at[i, m, 0:size, :], r_ss.at[3 * i + m], r_rs.at[3 * i + m],
                *at(0, dy, dx, 0)
            )
            copy.start()
            shares.append(copy)

    early = half * 2 // 3 // 16 * 16
    hops = []
    for q in range(4):
        source = summed.at[pl.ds(pl.multiple_of(chunk * far[2] + half * q, 16), early), :]
        place = zin.at[half * q : half * q + early, :]
        hops.append(remote(source, place, zn_ss.at[q], zn_rs.at[q], far[2] * 2 + y, s))
    for i, zd in enumerate(order):
        pairs[i].wait_recv()

        def add_pair(m, carry, zd=zd):
            here = pl.ds(pl.multiple_of(zd * chunk + m * part, part), part)
            summing = terms[here, :] + pair_in[here, :].astype(F32)
            terms[here, :] = summing
            summed[here, :] = summing.astype(BF16)
            return carry

        lax.fori_loop(0, steps, add_pair, 0)
        if i == 1:
            for hop in hops:
                send(hop)
        elif i < zs - 1:
            plane_send(i // 2, zd)
    plane_send(zs - 2, far[2], early)

    def rescale(t, carry):
        factor = facts[pl.ds(t, 1), :]
        for r in range(rows):
            for b in range(3):
                tap = slice(b * ch, (b + 1) * ch)
                scaled[t, r + 1, :, tap] = (gcat[t * rows + r, :, tap].astype(F32) * factor).astype(BF16)
        return carry

    w_cross(1)
    w_cross(0)
    lax.fori_loop(0, slots, rescale, 0)
    remote(other_block(1 - core), other_block(1 - core), sw_ss.at[zs - 1], sw_rs.at[z], *sibling).wait_recv()
    for j in (2, 1, 0):
        place = group(far[j], 1 - core)
        remote(place, place, sw_ss.at[j], sw_rs.at[far[j]], *sibling).wait_recv()

    def sums(k, dots):
        here = pl.ds(pl.multiple_of(k * part, part), part)
        wv = jnp.concatenate([wfull[0, here, :], wfull[1, here, :]], axis=1).astype(F32)
        return tuple(dots[t] + fold(wv * mains[t, here, :]) for t in range(slots))

    zero = jnp.zeros((8, ch), F32)
    dots = lax.fori_loop(0, 9 * ch // part, sums, (zero,) * slots)
    for t in range(slots):
        pull = live[t] * demod[t] * demod[t] * demod[t] * jnp.sum(dots[t], axis=0, keepdims=True) * scale
        pull_all[s, d, t : t + 1, :] = pull[:, :lanes]
        pull_all[s, d, slots + t : slots + t + 1, :] = pull[:, lanes:]
    spread(pull_all, pl_ss, pl_rs)

    for way, (_, _, takes) in enumerate(ways):
        @pl.when(takes)
        def _(way=way):
            halos[way][1].wait_recv()

    def edges():
        for t in range(slots):
            for b in range(3):
                tap = slice(b * ch, (b + 1) * ch)
                above, factor = (slots * rows, hdem_in[0, 0:1, :]) if t == 0 else (t * rows - 1, demod[t - 1])
                scaled[t, 0, :, tap] = (gcat[above, :, tap].astype(F32) * (factor * top_on[t])).astype(BF16)
                below = gcat[slots * rows + 1, :, tap].astype(F32) * (hdem_in[1, 0:1, :] * last_on[t])
                if t < slots - 1:
                    below = below + gcat[(t + 1) * rows, :, tap].astype(F32) * (demod[t + 1] * next_on[t])
                scaled[t, rows + 1, :, tap] = below.astype(BF16)
        for a in range(3):
            for b in range(3):
                tap = 3 * a + b
                for h in range(2):
                    wcat[a, :, b * ch + h * lanes : b * ch + (h + 1) * lanes] = wfull[h, tap * ch : (tap + 1) * ch, :]

    def tile_back(t, carry):
        found = None
        for a in range(3):
            left = scaled[t, 2 - a : 2 - a + rows].reshape(rows * cols, 3 * ch)
            more = lax.dot_general(left, wcat[a], (((1,), (1,)), ((), ())), preferred_element_type=F32)
            found = more if found is None else found + more
        found = (found * style_ref[pl.ds(t, 1), :]).astype(BF16)
        tg_ref[t] = found.reshape(rows, cols, ch)
        return carry

    for q, hop in enumerate(hops):
        hop.wait_recv()
        here = pl.ds(pl.multiple_of(chunk * z + half * q, 16), early)
        summing = terms[here, :] + zin[half * q : half * q + early, :].astype(F32)
        terms[here, :] = summing
        summed[here, :] = summing.astype(BF16)
    plane_send(zs - 1, z)
    edges()
    lines = []
    for i, zd in enumerate([far[0], far[1], far[2], z]):
        low = early if i == zs - 2 else 0
        size = half - low
        own = terms[share(zd, 0, 0, low), :]
        for m in range(3):
            shares[3 * i + m].wait_recv()
            own = own + rs_in[i, m, 0:size, :].astype(F32)
        if i < zs - 1:
            line_out[i, 0:size, :] = own.astype(BF16)
            place = line_in.at[z, 0:size, :]
            lines.append(remote(line_out.at[i, 0:size, :], place, l_ss.at[i], l_rs.at[z], zd * 2 + y, s))
            lines[-1].start()
        if i == zs - 2:
            lax.fori_loop(0, slots - 2, tile_back, 0)
            collect(pull_all, pl_ss, pl_rs)
            for k in range(1, secs):
                send(remote(pull_all.at[s], pull_all.at[s], px_ss.at[k - 1], px_rs.at[k - 1], d, (s + k) % secs))
            lax.fori_loop(slots - 2, slots, tile_back, 0)
    for j in (2, 1, 0):
        size = half - early if j == 2 else half
        place = line_in.at[far[j], 0:size, :]
        remote(line_out.at[j, 0:size, :], place, l_ss.at[j], l_rs.at[far[j]], far[j] * 2 + y, s).wait_recv()
        more = line_in[far[j], 0:size, :].astype(F32)
        own = jnp.concatenate([own[:early], own[early:] + more], axis=0) if j == 2 else own + more
    fin[s] = own.astype(BF16)
    gathers = []
    for k in range(1, secs):
        copy = remote(fin.at[s], fin.at[s], a_ss.at[k - 1], a_rs.at[k - 1], d, (s + k) % secs)
        copy.start()
        gathers.append(copy)

    for k in range(1, secs):
        for ref, ss, rs in ((sq_all, sx_ss, sx_rs), (pull_all, px_ss, px_rs)):
            place = ref.at[(s + secs - k) % secs]
            remote(place, place, ss.at[k - 1], rs.at[k - 1], d, (s + k) % secs).wait_recv()
    tall = secs * wide
    upper = lax.broadcasted_iota(jnp.int32, (tall, lanes), 0) % (2 * slots) < slots

    def unpacked(ref):
        value = ref[...].reshape(tall, lanes)
        moved = pltpu.roll(value, tall - slots, 0)
        return jnp.concatenate([jnp.where(upper, value, 0.0), jnp.where(upper, moved, 0.0)], axis=1)

    coupled = jnp.dot(
        unpacked(sq_all).T, unpacked(pull_all), precision=lax.Precision.HIGHEST, preferred_element_type=F32
    )
    coup[0:ch, :] = coupled
    coup[ch : 2 * ch, :] = coupled
    for q in range(secs):
        row, h = half * (q // 2), q % 2
        w_own = wfull[h, pl.ds(pl.multiple_of(block * d + row, 16), half), :].astype(F32)
        c_own = coup[pl.ds(pl.multiple_of(shift + row, 16), half), h * lanes : (h + 1) * lanes]
        wg_ref[row : row + half, h * lanes : (h + 1) * lanes] = w_own * c_own
    for k in range(1, secs):
        other = fin.at[(s + secs - k) % secs]
        remote(other, other, a_ss.at[k - 1], a_rs.at[k - 1], d, (s + k) % secs).wait_recv()
    for q in range(secs):
        row, h = half * (q // 2), q % 2
        span = (slice(row, row + half), slice(h * lanes, (h + 1) * lanes))
        wg_ref[span] = fin[q].astype(F32) - wg_ref[span]
    for way, (_, gives, _) in enumerate(ways):
        @pl.when(gives)
        def _(way=way):
            for copy in halos[way]:
                copy.wait_send()

    for copy in sends + pairs + shares + lines + gathers:
        copy.wait_send()


def store_kernel(tg_ref, wg_ref, tg_out, wg_out, t_sem, w_sem):
    copies = [pltpu.make_async_copy(tg_ref.at[t], tg_out.at[t], t_sem.at[t]) for t in range(tg_ref.shape[0])]
    copies.append(pltpu.make_async_copy(wg_ref, wg_out, w_sem))
    for copy in copies:
        copy.start()
    for copy in copies:
        copy.wait()


def fused(dps, secs, tiles, out_grad, style, weight, tile_counts, crop_first):
    slots, rows, cols, ch = tiles.shape
    block = weight.shape[0]
    half = block // 2
    lanes = ch // 2
    zs = dps // 2
    scale = 1.0 / (slots * dps * secs * rows * cols) ** 0.5
    dma = pltpu.SemaphoreType.DMA
    vmem = pl.BlockSpec(memory_space=pltpu.VMEM)
    hbm = pl.BlockSpec(memory_space=pltpu.HBM)
    counts = [dps - 1, dps, secs - 1, secs - 1, dps - 1, dps, dps - 1, dps, secs - 1, secs - 1]
    counts += [zs - 1, zs, 1, 1, 3 * zs - 3, 3 * zs, zs, zs, zs, zs, 3 * zs, 3 * zs, zs - 1, zs, 4, 4, secs - 1, secs - 1]
    tg, wg = pl.pallas_call(
        functools.partial(fused_kernel, dps, secs, scale),
        out_shape=(
            pltpu.VMEM(tiles.shape, BF16),
            pltpu.VMEM(weight.shape, F32),
        ),
        in_specs=[hbm] * 6,
        out_specs=(vmem, vmem),
        scratch_shapes=[
            pltpu.SMEM(tile_counts.shape, jnp.int32),
            pltpu.SMEM(crop_first.shape, jnp.int32),
            pltpu.VMEM(tiles.shape, BF16),
            pltpu.VMEM(tiles.shape, BF16),
            pltpu.VMEM(style.shape, F32),
            pltpu.VMEM((2, 9 * ch, lanes), BF16),
            pltpu.VMEM((2, 2, cols, ch), BF16),
            pltpu.VMEM((2, 2, cols, ch), BF16),
            pltpu.VMEM((2, 8, ch), F32),
            pltpu.VMEM((2, 8, ch), F32),
            pltpu.VMEM((2 * ch, ch), F32),
            pltpu.VMEM((secs, dps, 2 * slots, lanes), F32),
            pltpu.VMEM((dps, 2 * slots, lanes), F32),
            pltpu.VMEM((dps, 2 * slots, lanes), F32),
            pltpu.VMEM((secs, dps, 2 * slots, lanes), F32),
            pltpu.VMEM((2 * ch, ch), F32),
            pltpu.VMEM((slots, ch, (rows + 2) * cols), BF16),
            pltpu.VMEM((slots * rows + 2, cols, 3 * ch), BF16),
            pltpu.VMEM((slots, 9 * ch, ch), F32),
            pltpu.VMEM((3, ch, 3 * ch), BF16),
            pltpu.VMEM((slots, rows + 2, cols, 3 * ch), BF16),
            pltpu.VMEM((8, ch), F32),
            pltpu.VMEM((9 * ch, lanes), F32),
            pltpu.VMEM((9 * ch, lanes), BF16),
            pltpu.VMEM((9 * ch, lanes), BF16),
            pltpu.VMEM((9 * ch, lanes), BF16),
            pltpu.VMEM((zs, 3, half, lanes), BF16),
            pltpu.VMEM((zs - 1, half, lanes), BF16),
            pltpu.VMEM((zs, half, lanes), BF16),
            pltpu.VMEM((2 * block, lanes), BF16),
            pltpu.VMEM((secs, half, lanes), BF16),
            dma((7,)), dma((4,)), dma((4,)),
        ] + [dma((count,)) for count in counts],
        compiler_params=pltpu.CompilerParams(collective_id=0, has_side_effects=True, vmem_limit_bytes=56 * 1024 * 1024),
        name="fused_backward",
    )(tile_counts, crop_first, tiles, out_grad, style, weight)
    return pl.pallas_call(
        store_kernel,
        out_shape=(
            jax.ShapeDtypeStruct(tiles.shape, BF16),
            jax.ShapeDtypeStruct(weight.shape, F32),
        ),
        in_specs=[vmem, vmem],
        out_specs=(hbm, hbm),
        scratch_shapes=[dma((slots,)), dma],
        compiler_params=pltpu.CompilerParams(has_side_effects=True, vmem_limit_bytes=1024 * 1024),
        name="store_out",
    )(tg, wg)


def solution(mesh):
    placed = (
        P(("dp", "section"), None, None, None),
        P(("dp", "section"), None, None, None),
        P(("dp", "section"), None),
        P("dp", None),
        P(("dp", "section")),
        P(("dp", "section")),
    )
    dps, secs = mesh.shape["dp"], mesh.shape["section"]

    def body(tiles, out_grad, style, weight, tile_counts, crop_first):
        args = (tiles, out_grad, style, weight, tile_counts, crop_first)
        rows, ch = weight.shape
        if secs == 4 and dps == 8 and tiles.shape[0] == 4 and rows % 32 == 0 and ch <= rows < 2 * ch:
            return fused(dps, secs, *args)
        return per_device(*args)

    return jax.shard_map(
        body,
        mesh=mesh,
        in_specs=placed,
        out_specs=(P(("dp", "section"), None, None, None), P("dp", None)),
        check_vma=False,
    )
```
